128 devices in a mesh: dp: 8 (over z_lo, x), expert: 16 (over z_hi, y, core).
Axes of the slice: x: 4, y: 4, z: 4 (z_hi: 2, z_lo: 2; z = z_hi * 2 + z_lo), core: 2. Of those that a mesh axis runs over, the one named last changes fastest.
Arguments:
- tokens: bfloat16 [196608, 2048], P(('dp', 'expert')), may hold values from -6 to 6
- upstream: bfloat16 [196608, 2048], P(('dp', 'expert')), may hold values from -6 to 6
- counts: int32 [2048], P(('dp', 'expert')), may hold values from 1 to 96, 122880 in all
- assign: int32 [2, 16], replicated, may hold values from 0 to 31
- gate_weight: bfloat16 [32, 512, 2048], P(None, 'expert', 'dp'), may hold values from -0.125 to 0.125
- up_weight: bfloat16 [32, 512, 2048], P(None, 'expert', 'dp'), may hold values from -0.125 to 0.125
- down_weight: bfloat16 [32, 512, 2048], P(None, 'expert', 'dp'), may hold values from -0.25 to 0.25
Outputs:
- token_grad: bfloat16 [196608, 2048], P(('dp', 'expert'))
- gate_weight_grad: float32 [32, 512, 2048], P(None, 'expert', 'dp')
- up_weight_grad: float32 [32, 512, 2048], P(None, 'expert', 'dp')
- down_weight_grad: float32 [32, 512, 2048], P(None, 'expert', 'dp')
The draws below stay inside these ranges and needn't reach their ends.
Inputs may be any that keep to these rules, and one draw needn't show every extreme that they name: assign[s, i] is the expert used by copy slot i in microstep s; several slots may use the same expert. counts[j] live leading rows in micro-batch j of 96 slots; some micro-batch is full in every draw.
All inputs are finite; a program needn't handle non-finite values. No bound on the sum of `counts` on one device may be relied on, other than what follows from the above.
Results may differ from the reference program's by a relative error of at most 0.012.
Values may be sent and summed in bfloat16 or wider, within the bound.
A program may use at most 128 MiB of HBM per device.

```python
import math
import jax
import jax.numpy as jnp
import numpy as np
from jax import lax

D = 2048
FF = 512
MICRO = 8
STEPS = 2
ROWS = 96
GROUPS = 16
EXPERTS = 32
TOKENS = 196608
DEVICES = 128


def set_ends(result, key, low, top_value):
    index_at = [jax.random.randint(jax.random.fold_in(key, axis), (), 0, length) for axis, length in enumerate(result.shape)]
    main_axis = result.shape.index(max(result.shape))
    neighbour = index_at[:main_axis] + [(index_at[main_axis] + 1) % result.shape[main_axis]] + index_at[main_axis + 1:]
    return result.at[tuple(index_at)].set(low).at[tuple(neighbour)].set(top_value)


def shard_levels(stream_key, extent, pieces, least, largest):
    loudness, own = 1.0, jax.random.fold_in(stream_key, 6)
    for axis_at, shards_of in pieces:
        draws = jnp.exp(jax.random.uniform(jax.random.fold_in(own, axis_at), (shards_of,), jnp.float32, least / len(pieces), largest / len(pieces)))
        loudness = loudness * jnp.repeat(draws, extent[axis_at] // shards_of).reshape([-1 if axis == axis_at else 1 for axis in range(len(extent))])
    return loudness


def length_profile(count, total, reach, lean):
    loads = [(1 << 20) // math.isqrt(grade ** lean) + 1 for grade in range(2, count + 1)]
    rest, given = total - reach - (count - 1), [1] * (count - 1)
    while rest > 0:
        movable = [i for i in range(count - 1) if given[i] < reach]
        mass, remaining = sum([loads[i] for i in movable]), rest
        for i in movable:
            addition = min(reach - given[i], max(1, remaining * loads[i] // mass), rest)
            given[i] = given[i] + addition
            rest = rest - addition
    return np.array([reach] + given)


def ragged_sizes(key, amount, total, reach, slope):
    if amount == 2:
        one = jax.random.randint(key, (), max(1, total - reach), min(reach, total - 1) + 1)
        return jnp.stack([one, total - one])
    tallies = jnp.asarray(length_profile(amount, total, reach, slope), jnp.int32)
    twos = (amount - 1) // 2
    donor, sink = tallies[1:1 + 2 * twos:2], tallies[2:2 + 2 * twos:2]
    slack = jnp.minimum(donor - 1, reach - sink)
    passed = jax.random.randint(jax.random.fold_in(key, 1), (twos,), 0, 1 << 20) % (slack + 1)
    tallies = tallies.at[1:1 + 2 * twos:2].set(donor - passed).at[2:2 + 2 * twos:2].set(sink + passed)
    return tallies[jax.random.permutation(jax.random.fold_in(key, 2), amount)]


def centred(key, dims, deviation, most, pieces=(), kind=jnp.bfloat16):
    entries = jax.random.normal(key, dims, jnp.float32) * deviation
    if len(pieces) > 0:
        entries = shard_levels(key, dims, pieces, -0.22, 0.18) * entries
    return jnp.clip(entries, min=-most, max=most).astype(kind)


def setup_inputs(seed: int = 0) -> dict:
    key_of = jax.random.split(jax.random.key(seed), 8)
    return {
        "tokens": centred(key_of[0], (TOKENS, D), 1.0, 6.0, ((0, 128),)),
        "upstream": centred(key_of[1], (TOKENS, D), 1.0, 6.0, ((0, 128),)),
        "counts": ragged_sizes(key_of[2], DEVICES * STEPS * MICRO, DEVICES * STEPS * MICRO * ROWS * 5 // 8, ROWS, 2).astype(jnp.int32),
        "assign": set_ends(jax.random.randint(key_of[3], (STEPS, GROUPS), 0, EXPERTS), jax.random.fold_in(key_of[3], 1), 0, EXPERTS - 1).astype(jnp.int32),
        "gate_weight": centred(key_of[4], (EXPERTS, FF, D), D ** -0.5, 0.125, ((1, 16), (2, 8))),
        "up_weight": centred(key_of[5], (EXPERTS, FF, D), D ** -0.5, 0.125, ((1, 16), (2, 8))),
        "down_weight": centred(key_of[6], (EXPERTS, FF, D), FF ** -0.5, 0.25, ((1, 16), (2, 8))),
    }


def expert_backward(token_rows, upstream_rows, live_rows, gate_full, up_full, down_full, grad_scale):
    contract_last = (((1,), (1,)), ((), ()))
    contract_first = (((0,), (0,)), ((), ()))
    gate_pre = lax.dot_general(token_rows, gate_full, contract_last, preferred_element_type=jnp.float32)
    up_pre = lax.dot_general(token_rows, up_full, contract_last, preferred_element_type=jnp.float32)
    sigmoid = jax.nn.sigmoid(gate_pre)
    active = gate_pre * sigmoid
    hidden = (active * up_pre).astype(jnp.bfloat16)
    masked = jnp.where(live_rows[:, None], upstream_rows, jnp.zeros_like(upstream_rows))
    hidden_grad = lax.dot_general(masked, down_full, contract_last, preferred_element_type=jnp.float32)
    gate_grad = (hidden_grad * up_pre * sigmoid * (1.0 + gate_pre * (1.0 - sigmoid))).astype(jnp.bfloat16)
    up_grad = (hidden_grad * active).astype(jnp.bfloat16)
    input_grad = jnp.dot(gate_grad, gate_full, preferred_element_type=jnp.float32) + jnp.dot(up_grad, up_full, preferred_element_type=jnp.float32)
    gate_term = lax.dot_general(gate_grad, token_rows, contract_first, preferred_element_type=jnp.float32) * grad_scale
    up_term = lax.dot_general(up_grad, token_rows, contract_first, preferred_element_type=jnp.float32) * grad_scale
    down_term = lax.dot_general(hidden, masked, contract_first, preferred_element_type=jnp.float32) * grad_scale
    return input_grad.astype(jnp.bfloat16), gate_term, up_term, down_term


def round_trip(value):
    return lax.optimization_barrier(value.astype(jnp.bfloat16)).astype(jnp.float32)


def reference(tokens, upstream, counts, assign, gate_weight, up_weight, down_weight):
    block_rows = MICRO * ROWS
    grad_scale = 1.0 / block_rows
    token_blocks = tokens.reshape(DEVICES, STEPS, block_rows, D)
    upstream_blocks = upstream.reshape(DEVICES, STEPS, block_rows, D)
    count_blocks = counts.reshape(DEVICES, STEPS, MICRO)
    device_slot = (jnp.arange(DEVICES, dtype=jnp.int32) % GROUPS).astype(jnp.int32)
    position = jnp.arange(ROWS, dtype=jnp.int32)

    def visit_device(totals, inputs):
        token_dev, upstream_dev, count_dev, slot_index = inputs
        gate_total, up_total, down_total = totals
        produced = []
        for micro_step in range(STEPS):
            chosen = assign[micro_step, slot_index].astype(jnp.int32)
            live_rows = (position[None, :] < count_dev[micro_step][:, None]).reshape(block_rows)
            input_grad, gate_term, up_term, down_term = expert_backward(
                token_dev[micro_step], upstream_dev[micro_step], live_rows,
                gate_weight[chosen], up_weight[chosen], down_weight[chosen], grad_scale)
            gate_total = gate_total.at[chosen].add(round_trip(gate_term))
            up_total = up_total.at[chosen].add(round_trip(up_term))
            down_total = down_total.at[chosen].add(round_trip(down_term))
            produced.append(input_grad)
        return (gate_total, up_total, down_total), jnp.stack(produced)

    empty_grad = jnp.zeros((EXPERTS, FF, D), jnp.float32)
    totals, token_grad = lax.scan(visit_device, (empty_grad, empty_grad, empty_grad),
                                  (token_blocks, upstream_blocks, count_blocks, device_slot))
    return token_grad.reshape(TOKENS, D), totals[0], totals[1], totals[2]
```

```python
import functools

import jax
import jax.numpy as jnp
from jax import lax
from jax.experimental import pallas as pl
from jax.experimental.pallas import tpu as pltpu
from jax.sharding import PartitionSpec as P

MESH = pl.DeviceIdType.MESH
F32 = jnp.float32
BF16 = jnp.bfloat16
NT = (((1,), (1,)), ((), ()))
NN = (((1,), (0,)), ((), ()))

NA = 9
HA = 5
HB = 3
VMEM_BYTES = 67043328


def fused_kernel(cfg, assign_ref, live_ref, tok_ref, ups_ref, gate_ref, up_ref, down_ref,
                 tg_out, recv_out,
                 stage, wfull, part, rz, rhla, rhlb, rhra, rhrb, rfla, rflb, rfra, rfrb, rza,
                 xg, acc, t3, gn, tg,
                 w_send, w_recv, g_send, g_recv, ag_send, ag_recv, rs_send, rs_recv,
                 xg_sem, tg_sem, own_sem):
    G, NX, steps, block, rows, width, units = cfg
    NB = units - NA
    half = units // 2
    hrows = half * rows
    dp = lax.axis_index("dp")
    g = lax.axis_index("expert")
    x = dp % NX
    z = dp // NX
    zh = g // half
    right = (x + 1) % NX
    left = (x + NX - 1) % NX
    opp = (x + 2) % NX
    zz = 1 - z
    pS, pL, pR, pO = z * NX + x, z * NX + left, z * NX + right, z * NX + opp
    qS, qL, qR, qO = zz * NX + x, zz * NX + left, zz * NX + right, zz * NX + opp
    dev_r = {"dp": pR, "expert": g}
    dev_l = {"dp": pL, "expert": g}
    dev_z = {"dp": qS, "expert": g}

    A = pl.ds(0, NA)
    A1 = pl.ds(0, HA)
    A2 = pl.ds(HA, NA - HA)
    B = pl.ds(NA, NB)
    B1 = pl.ds(NA, HB)
    B2 = pl.ds(NA + HB, NB - HB)

    def peer(j):
        gp = (g + j) % G
        zp = (z + zh + gp // half) % 2
        return gp, {"dp": zp * NX + x, "expert": gp}

    barrier = pltpu.get_barrier_semaphore()

    def greet(j, carry):
        pl.semaphore_signal(barrier, inc=1, device_id=peer(j)[1], device_id_type=MESH)
        return carry

    lax.fori_loop(1, G, greet, 0)
    for dev in (dev_r, dev_l, dev_z):
        pl.semaphore_signal(barrier, inc=1, device_id=dev, device_id_type=MESH)

    def load_xg(s):
        def one(d, carry):
            cols = pl.ds(pl.multiple_of(d * width, width), width)
            for k, ref in enumerate((tok_ref, ups_ref)):
                pltpu.make_async_copy(ref.at[pl.ds(s * block, block), cols], xg.at[k, d], xg_sem.at[s]).start()
            return carry

        lax.fori_loop(0, 2 * NX, one, 0)

    def wait_xg(s):
        pltpu.make_async_copy(xg, xg, xg_sem.at[s]).wait()

    load_xg(0)

    def pick(s):
        def one(i, carry):
            c = assign_ref[s, i]
            stage[s, i, 0] = gate_ref[c]
            stage[s, i, 1] = up_ref[c]
            stage[s, i, 2] = down_ref[c]
            return carry

        lax.fori_loop(0, G, one, 0)
        wfull[s, pS, g] = stage[s, g]

    pick(0)
    pl.semaphore_wait(barrier, G - 1 + 3)

    def spread(s):
        def one(j, carry):
            gp, dev = peer(j)
            pltpu.make_async_remote_copy(
                stage.at[s, gp], wfull.at[s, dev["dp"], g], w_send.at[s], w_recv.at[s],
                device_id=dev, device_id_type=MESH).start()
            return carry

        lax.fori_loop(1, G, one, 0)

    def spread_wait(s):
        few = pl.ds(0, G - 1)
        pltpu.make_async_copy(stage.at[s, few], stage.at[s, few], w_recv.at[s]).wait()

    pending = []

    def send(src, dst, ssem, rsem, dev):
        copy = pltpu.make_async_remote_copy(src, dst, ssem, rsem, device_id=dev, device_id_type=MESH)
        copy.start()
        pending.append(copy)
        return copy

    class Gather:
        def __init__(self, s):
            self.s = s
            self.c = {}

        def go(self, k, p, piece, dev):
            ref = wfull.at[self.s, p, piece]
            self.c[k] = send(ref, ref, ag_send.at[self.s, k], ag_recv.at[self.s, k], dev)

        def first(self):
            spread_wait(self.s)
            self.go(0, pS, B, dev_r)
            self.go(1, pS, B, dev_l)
            self.go(2, pS, A, dev_z)
            self.go(3, pS, A, dev_r)
            self.go(4, pS, A, dev_l)
            self.go(5, pS, B, dev_z)

        def w(self, *ks):
            for k in ks:
                self.c[k].wait_recv()

        def relay_b(self):
            self.w(0)
            self.go(6, pL, B1, dev_r)
            self.go(10, pL, B, dev_z)
            self.w(1)
            self.go(7, pR, B2, dev_l)
            self.go(11, pR, B, dev_z)

        def partner_a(self):
            self.w(2)
            self.go(8, qS, A, dev_r)
            self.go(9, qS, A, dev_l)

        def relay_a(self):
            self.w(3)
            self.go(12, pL, A1, dev_r)
            self.w(4)
            self.go(13, pR, A2, dev_l)

        def opp_b(self):
            self.w(6)
            self.go(16, pO, B1, dev_z)
            self.w(7)
            self.go(17, pO, B2, dev_z)

        def relay_pa(self):
            self.w(8)
            self.go(14, qL, A1, dev_r)
            self.w(9)
            self.go(15, qR, A2, dev_l)

    def add_into(dst, *others):
        total = dst[...].astype(F32)
        for o in others:
            total = total + o[...].astype(F32)
        dst[...] = total.astype(BF16)

    def add_units(n, dst, *others):
        def one(i, carry):
            add_into(dst(i), *[o(i) for o in others])
            return carry

        lax.fori_loop(0, n, one, 0)

    class Reduce:
        def __init__(self, s):
            self.s = s
            self.c = {}

        def go(self, k, src, dst, dev):
            self.c[k] = send(src, dst, rs_send.at[self.s, k], rs_recv.at[self.s, k], dev)

        def w(self, *ks):
            for k in ks:
                self.c[k].wait_recv()

        def first(self):
            s = self.s
            pt = part.at[s]
            self.go(0, pt.at[qO, A1], rhla.at[s, 1], dev_r)
            self.go(1, pt.at[qO, A2], rhra.at[s, 1], dev_l)
            self.go(2, pt.at[qO, B], rz.at[s, 2], dev_z)
            self.go(3, pt.at[pO, A1], rhla.at[s, 0], dev_r)
            self.go(4, pt.at[pO, A2], rhra.at[s, 0], dev_l)

        def first_z(self):
            s = self.s
            pt = part.at[s]
            self.go(5, pt.at[qR, B], rz.at[s, 1], dev_z)
            self.go(6, pt.at[qL, B], rz.at[s, 3], dev_z)
            self.go(7, pt.at[qS, B], rz.at[s, 0], dev_z)

        def mid_q(self):
            s = self.s
            pt = part.at[s]
            self.w(0)
            add_units(HA, lambda i: pt.at[qR, i], lambda i: rhla.at[s, 1, i])
            self.go(8, pt.at[qR, A], rfla.at[s, 1], dev_r)
            self.w(1)
            add_units(NA - HA, lambda i: pt.at[qL, HA + i], lambda i: rhra.at[s, 1, i])
            self.go(9, pt.at[qL, A], rfra.at[s, 1], dev_l)

        def opp_b(self):
            s = self.s
            pt = part.at[s]
            self.w(2)
            add_units(NB, lambda i: pt.at[pO, NA + i], lambda i: rz.at[s, 2, i])
            self.go(10, pt.at[pO, B1], rhlb.at[s], dev_r)
            self.go(11, pt.at[pO, B2], rhrb.at[s], dev_l)

        def mid_p(self):
            s = self.s
            pt = part.at[s]
            self.w(3)
            add_units(HA, lambda i: pt.at[pR, i], lambda i: rhla.at[s, 0, i])
            self.go(12, pt.at[pR, A], rfla.at[s, 0], dev_r)
            self.w(4)
            add_units(NA - HA, lambda i: pt.at[pL, HA + i], lambda i: rhra.at[s, 0, i])
            self.go(13, pt.at[pL, A], rfra.at[s, 0], dev_l)

        def mid_b(self):
            s = self.s
            pt = part.at[s]
            self.w(5, 10)
            add_units(HB, lambda i: pt.at[pR, NA + i], lambda i: rz.at[s, 1, i], lambda i: rhlb.at[s, i])
            add_units(NB - HB, lambda i: pt.at[pR, NA + HB + i], lambda i: rz.at[s, 1, HB + i])
            self.go(14, pt.at[pR, B], rflb.at[s], dev_r)
            self.w(6, 11)
            add_units(HB, lambda i: pt.at[pL, NA + i], lambda i: rz.at[s, 3, i])
            add_units(NB - HB, lambda i: pt.at[pL, NA + HB + i], lambda i: rz.at[s, 3, HB + i], lambda i: rhrb.at[s, i])
            self.go(15, pt.at[pL, B], rfrb.at[s], dev_l)

        def to_partner(self):
            s = self.s
            pt = part.at[s]
            self.w(8, 9)
            add_units(NA, lambda i: pt.at[qS, i], lambda i: rfla.at[s, 1, i], lambda i: rfra.at[s, 1, i])
            self.go(16, pt.at[qS, A], rza.at[s], dev_z)

        def finish(self):
            s = self.s
            pt = part.at[s]
            self.w(7, 14, 15)
            add_units(NB, lambda i: pt.at[pS, NA + i], lambda i: rz.at[s, 0, i], lambda i: rflb.at[s, i], lambda i: rfrb.at[s, i])
            self.w(12, 13, 16)
            add_units(NA, lambda i: pt.at[pS, i], lambda i: rfla.at[s, 0, i], lambda i: rfra.at[s, 0, i], lambda i: rza.at[s, i])

            def one(j, carry):
                gp, dev = peer(j)
                pltpu.make_async_remote_copy(
                    pt.at[pS, gp], recv_out.at[s, g], g_send.at[s], g_recv.at[s],
                    device_id=dev, device_id_type=MESH).start()
                return carry

            lax.fori_loop(1, G, one, 0)
            pltpu.make_async_copy(pt.at[pS, g], recv_out.at[s, g], own_sem.at[s]).start()

        def done(self):
            s = self.s
            few = pl.ds(0, G - 1)
            pltpu.make_async_copy(recv_out.at[s, few], recv_out.at[s, few], g_recv.at[s]).wait()
            pltpu.make_async_copy(part.at[s, pS, 0], recv_out.at[s, 0], own_sem.at[s]).wait()

    def shard_of(p, h):
        return ((p // NX + h + zh) % 2) * NX + p % NX

    def weight(s, p, h, m):
        return wfull[s, p, pl.ds(h * half, half), m].reshape(hrows, width)

    def forward(s, p, start=False):
        def one(j, carry):
            m, h = j // 2, j % 2
            got = lax.dot_general(weight(s, p, h, m), xg[m // 2, shard_of(p, h)], NT, preferred_element_type=F32)
            if start:
                acc[m, h] = got
            else:
                acc[m, h] += got
            return carry

        lax.fori_loop(0, 6, one, 0)

    def gates(s):
        live = live_ref[s] > 0.5
        tall = 32

        def one(j, carry):
            h = j // (hrows // tall)
            at = pl.ds(pl.multiple_of((j % (hrows // tall)) * tall, tall), tall)
            pre = acc[0, h, at, :]
            upv = acc[1, h, at, :]
            hg = jnp.where(live, acc[2, h, at, :], 0.0)
            sig = jax.nn.sigmoid(pre)
            act = pre * sig
            t3[0, h, at, :] = (hg * upv * sig * (1.0 + pre * (1.0 - sig))).astype(BF16)
            t3[1, h, at, :] = (hg * act).astype(BF16)
            t3[2, h, at, :] = jnp.where(live, act * upv, 0.0).astype(BF16)
            return carry

        lax.fori_loop(0, 2 * (hrows // tall), one, 0)

    scale = 1.0 / block

    def parts(s, p):
        def one(j, carry):
            m, h = j // 2, j % 2
            got = lax.dot_general(t3[m, h], xg[m // 2, shard_of(p, h)], NN, preferred_element_type=F32) * scale
            part[s, p, pl.ds(h * half, half), m] = got.astype(BF16).reshape(half, rows, width)
            return carry

        lax.fori_loop(0, 6, one, 0)

    def turn():
        def one(j, carry):
            gn[j // 2, j % 2] = t3[j // 2, j % 2].T
            return carry

        lax.fori_loop(0, 4, one, 0)

    def tg_copy(s, d):
        cols = pl.ds(pl.multiple_of(d * width, width), width)
        return pltpu.make_async_copy(tg.at[d], tg_out.at[pl.ds(s * block, block), cols], tg_sem.at[d])

    def token_grads(s, lo, hi):
        def one(d, carry):
            total = None
            for m in (0, 1):
                for h in (0, 1):
                    got = jnp.dot(gn[m, h], weight(s, shard_of(d, h), h, m), preferred_element_type=F32)
                    total = got if total is None else total + got
            tg[d] = total.astype(BF16)
            tg_copy(s, d).start()
            return carry

        lax.fori_loop(lo, hi, one, 0)

    def tg_wait(s):
        def one(d, carry):
            tg_copy(s, d).wait()
            return carry

        lax.fori_loop(0, 2 * NX, one, 0)

    g0, g1 = Gather(0), Gather(1)
    r0, r1 = Reduce(0), Reduce(1)

    spread(0)
    pick(1)
    g0.first()
    spread(1)
    wait_xg(0)
    forward(0, pS, start=True)
    g0.relay_b()
    g0.partner_a()
    g0.relay_a()
    forward(0, pL)
    forward(0, pR)
    g0.w(5)
    forward(0, qS)
    g0.opp_b()
    g0.relay_pa()
    g1.first()
    g0.w(10)
    forward(0, qL)
    g0.w(11)
    forward(0, qR)
    g0.w(12, 13)
    forward(0, pO)
    g0.w(14, 15, 16, 17)
    forward(0, qO)
    gates(0)
    g1.relay_b()
    g1.partner_a()
    parts(0, qO)
    parts(0, pO)
    parts(0, qR)
    parts(0, qL)
    g1.relay_a()
    parts(0, qS)
    parts(0, pR)
    parts(0, pL)
    parts(0, pS)
    load_xg(1)
    g1.opp_b()
    turn()
    token_grads(0, 0, 4)
    g1.relay_pa()
    r0.first()
    r0.first_z()
    token_grads(0, 4, 8)
    wait_xg(1)
    forward(1, pS, start=True)
    forward(1, pL)
    forward(1, pR)
    g1.w(5)
    forward(1, qS)
    g1.w(10)
    forward(1, qL)
    g1.w(11)
    forward(1, qR)
    g1.w(12, 13)
    forward(1, pO)
    g1.w(14, 15, 16, 17)
    forward(1, qO)
    gates(1)
    r0.mid_q()
    r0.opp_b()
    r0.mid_p()
    parts(1, qO)
    parts(1, pO)
    parts(1, qR)
    parts(1, qL)
    r0.mid_b()
    parts(1, qS)
    parts(1, pR)
    parts(1, pL)
    parts(1, pS)
    r0.to_partner()
    r1.first()
    r1.first_z()
    tg_wait(0)
    turn()
    token_grads(1, 0, 8)
    r0.finish()
    r1.mid_q()
    r1.opp_b()
    r1.mid_p()
    r1.mid_b()
    r1.to_partner()
    r1.finish()
    tg_wait(1)
    r0.done()
    r1.done()
    for copy in pending:
        copy.wait_send()
    for s in range(steps):
        few = pl.ds(0, G - 1)
        pltpu.make_async_copy(stage.at[s, few], stage.at[s, few], w_send.at[s]).wait()
        pltpu.make_async_copy(stage.at[s, few], stage.at[s, few], g_send.at[s]).wait()


def home_kernel(assign_ref, recv_ref, gate_ref, up_ref, down_ref):
    outs = (gate_ref, up_ref, down_ref)
    steps, count = recv_ref.shape[:2]
    for ref in outs:
        ref[...] = jnp.zeros_like(ref)

    def one(i, carry):
        s, k = i // count, i % count
        c = assign_ref[s, k]
        for m, ref in enumerate(outs):
            ref[c] += recv_ref[s, k, m].astype(F32)
        return carry

    lax.fori_loop(0, steps * count, one, 0)


def local(tokens, upstream, counts, assign, gate_weight, up_weight, down_weight):
    steps, G = assign.shape
    batch_count = counts.shape[0] // steps
    block = tokens.shape[0] // steps
    batch_rows = block // batch_count
    experts, rows, width = gate_weight.shape
    dp_count = tokens.shape[1] // width
    NX = dp_count // 2
    position = jnp.arange(batch_rows, dtype=jnp.int32)
    live = (position[None, :] < counts[:, None]).astype(F32).reshape(steps, 1, block)

    NB = G - NA
    unit = (3, rows, width)

    def vm(*shape, dtype=BF16):
        return pltpu.VMEM(shape, dtype)

    dma = pltpu.SemaphoreType.DMA
    half = G // 2
    hrows = half * rows
    scratch = [
        vm(steps, G, *unit),
        vm(steps, dp_count, G, *unit),
        vm(steps, dp_count, G, *unit),
        vm(steps, 4, NB, *unit),
        vm(steps, 2, HA, *unit),
        vm(steps, HB, *unit),
        vm(steps, 2, NA - HA, *unit),
        vm(steps, NB - HB, *unit),
        vm(steps, 2, NA, *unit),
        vm(steps, NB, *unit),
        vm(steps, 2, NA, *unit),
        vm(steps, NB, *unit),
        vm(steps, NA, *unit),
        vm(2, dp_count, block, width),
        vm(3, 2, hrows, block, dtype=F32),
        vm(3, 2, hrows, block),
        vm(2, 2, block, hrows),
        vm(dp_count, block, width),
        dma((steps,)), dma((steps,)), dma((steps,)), dma((steps,)),
        dma((steps, 18)), dma((steps, 18)), dma((steps, 17)), dma((steps, 17)),
        dma((steps,)), dma((dp_count,)), dma((steps,)),
    ]
    vmem = pl.BlockSpec(memory_space=pltpu.VMEM)
    smem = pl.BlockSpec(memory_space=pltpu.SMEM)
    anyw = pl.BlockSpec(memory_space=pl.ANY)
    cfg = (G, NX, steps, block, rows, width, G)
    flops = 2 * steps * 8 * block * (G * rows) * tokens.shape[1]
    token_grad, received = pl.pallas_call(
        functools.partial(fused_kernel, cfg),
        out_shape=(
            jax.ShapeDtypeStruct(tokens.shape, BF16),
            jax.ShapeDtypeStruct((steps, G, *unit), BF16),
        ),
        in_specs=[smem, vmem, anyw, anyw, vmem, vmem, vmem],
        out_specs=(anyw, anyw),
        scratch_shapes=scratch,
        compiler_params=pltpu.CompilerParams(
            collective_id=0, has_side_effects=True, vmem_limit_bytes=VMEM_BYTES
        ),
        cost_estimate=pl.CostEstimate(flops=flops, bytes_accessed=6 * tokens.size, transcendentals=0),
        name="expert_step",
    )(assign, live, tokens, upstream, gate_weight, up_weight, down_weight)

    grad = jax.ShapeDtypeStruct(gate_weight.shape, F32)
    grads = pl.pallas_call(
        home_kernel,
        out_shape=(grad, grad, grad),
        in_specs=[smem, vmem],
        out_specs=(vmem, vmem, vmem),
        name="to_experts",
    )(assign, received)
    return (token_grad, *grads)


def solution(mesh):
    placed = (
        P(("dp", "expert"), None),
        P(("dp", "expert"), None),
        P(("dp", "expert")),
        P(),
        P(None, "expert", "dp"),
        P(None, "expert", "dp"),
        P(None, "expert", "dp"),
    )
    return jax.shard_map(
        local,
        mesh=mesh,
        in_specs=placed,
        out_specs=(
            P(("dp", "expert"), None),
            P(None, "expert", "dp"),
            P(None, "expert", "dp"),
            P(None, "expert", "dp"),
        ),
        check_vma=False,
    )
```

```python
import functools

import jax
import jax.numpy as jnp
from jax import lax
from jax.experimental import pallas as pl
from jax.experimental.pallas import tpu as pltpu
from jax.sharding import PartitionSpec as P

MESH = pl.DeviceIdType.MESH
F32 = jnp.float32
BF16 = jnp.bfloat16
NT = (((1,), (1,)), ((), ()))
NN = (((1,), (0,)), ((), ()))

NB = 7
HB = 3
HA = 5
VMEM_BYTES = 67043328


def fused_kernel(cfg, assign_ref, counts_ref, tok_ref, ups_ref, gate_ref, up_ref, down_ref,
                 tg_out, recv_out,
                 stage, wfull, part, rz, rhla, rhlb, rhra, rhrb, rfla, rflb, rfra, rfrb, rza,
                 xg, acc, t3, gn, tg,
                 w_send, w_recv_b, w_recv_a, g_send, g_recv, ag_send, ag_recv, rs_send, rs_recv,
                 xg_sem, tg_sem, own_sem):
    G, NX, steps, block, rows, width, batches = cfg
    units = G
    batch_rows = block // batches
    NA = units - NB
    half = units // 2
    hrows = half * rows
    dp = lax.axis_index("dp")
    g = lax.axis_index("expert")
    x = dp % NX
    z = dp // NX
    zh = g // half
    right = (x + 1) % NX
    left = (x + NX - 1) % NX
    opp = (x + 2) % NX
    zz = 1 - z
    pS, pL, pR, pO = z * NX + x, z * NX + left, z * NX + right, z * NX + opp
    qS, qL, qR, qO = zz * NX + x, zz * NX + left, zz * NX + right, zz * NX + opp
    dev_r = {"dp": pR, "expert": g}
    dev_l = {"dp": pL, "expert": g}
    dev_z = {"dp": qS, "expert": g}

    B = pl.ds(0, NB)
    B1 = pl.ds(0, HB)
    B2 = pl.ds(HB, NB - HB)
    A = pl.ds(NB, NA)
    A1 = pl.ds(NB, HA)
    A2 = pl.ds(NB + HA, NA - HA)

    NY = half // 2
    y = (g // 2) % NY
    core = g % 2

    def peer(u, sign):
        k = (u % half) // 2
        dy = k + (k // 2) * (5 - 2 * k)
        far = u // half
        yp = (y + sign * dy + NY) % NY
        gp = ((zh + far) % 2) * half + yp * 2 + (core + u) % 2
        return gp, {"dp": ((z + far) % 2) * NX + x, "expert": gp}

    barrier = pltpu.get_barrier_semaphore()

    def greet(j, carry):
        pl.semaphore_signal(barrier, inc=1, device_id=peer(j, 1)[1], device_id_type=MESH)
        return carry

    lax.fori_loop(1, G, greet, 0)
    for dev in (dev_r, dev_l, dev_z):
        pl.semaphore_signal(barrier, inc=1, device_id=dev, device_id_type=MESH)

    def load_xg(s):
        def one(d, carry):
            cols = pl.ds(pl.multiple_of(d * width, width), width)
            for k, ref in enumerate((tok_ref, ups_ref)):
                pltpu.make_async_copy(ref.at[pl.ds(s * block, block), cols], xg.at[k, d], xg_sem.at[s]).start()
            return carry

        lax.fori_loop(0, 2 * NX, one, 0)

    def wait_xg(s):
        pltpu.make_async_copy(xg, xg, xg_sem.at[s]).wait()

    load_xg(0)

    def pick(s):
        def one(i, carry):
            c = assign_ref[s, i]
            stage[s, i, 0] = gate_ref[c]
            stage[s, i, 1] = up_ref[c]
            stage[s, i, 2] = down_ref[c]
            return carry

        lax.fori_loop(0, G, one, 0)
        wfull[s, pS, 0] = stage[s, g]

    pick(0)
    pl.semaphore_wait(barrier, G - 1 + 3)

    def spread(s):
        def one(u, carry, recv):
            gp, dev = peer(u, -1)
            pltpu.make_async_remote_copy(
                stage.at[s, gp], wfull.at[s, dev["dp"], u], w_send.at[s], recv.at[s],
                device_id=dev, device_id_type=MESH).start()
            return carry

        lax.fori_loop(1, NB, functools.partial(one, recv=w_recv_b), 0)
        lax.fori_loop(NB, G, functools.partial(one, recv=w_recv_a), 0)

    def bytes_of(count, sem):
        some = stage.at[0, pl.ds(0, count)]
        return pltpu.make_async_copy(some, some, sem)

    pending = []

    def send(src, dst, ssem, rsem, dev):
        copy = pltpu.make_async_remote_copy(src, dst, ssem, rsem, device_id=dev, device_id_type=MESH)
        copy.start()
        pending.append(copy)
        return copy

    class Gather:
        def __init__(self, s):
            self.s = s
            self.c = {}

        def go(self, k, p, piece, dev):
            ref = wfull.at[self.s, p, piece]
            self.c[k] = send(ref, ref, ag_send.at[self.s, k], ag_recv.at[self.s, k], dev)

        def first(self):
            bytes_of(NB - 1, w_recv_b.at[self.s]).wait()
            self.go(0, pS, B, dev_r)
            self.go(1, pS, B, dev_l)
            self.go(5, pS, B, dev_z)
            bytes_of(NA, w_recv_a.at[self.s]).wait()
            self.go(2, pS, A, dev_z)
            self.go(3, pS, A, dev_r)
            self.go(4, pS, A, dev_l)

        def w(self, *ks):
            for k in ks:
                self.c[k].wait_recv()

        def relay_b(self):
            self.w(0)
            self.go(6, pL, B1, dev_r)
            self.go(10, pL, B, dev_z)
            self.w(1)
            self.go(7, pR, B2, dev_l)
            self.go(11, pR, B, dev_z)

        def partner_a(self):
            self.w(2)
            self.go(8, qS, A, dev_r)
            self.go(9, qS, A, dev_l)

        def relay_a(self):
            self.w(3)
            self.go(12, pL, A1, dev_r)
            self.w(4)
            self.go(13, pR, A2, dev_l)

        def opp_b(self):
            self.w(6)
            self.go(16, pO, B1, dev_z)
            self.w(7)
            self.go(17, pO, B2, dev_z)

        def relay_pa(self):
            self.w(8)
            self.go(14, qL, A1, dev_r)
            self.w(9)
            self.go(15, qR, A2, dev_l)

    def add_into(dst, *others):
        total = dst[...].astype(F32)
        for o in others:
            total = total + o[...].astype(F32)
        dst[...] = total.astype(BF16)

    def add_units(n, dst, *others):
        def one(i, carry):
            add_into(dst(i), *[o(i) for o in others])
            return carry

        lax.fori_loop(0, n, one, 0)

    class Reduce:
        def __init__(self, s):
            self.s = s
            self.c = {}

        def go(self, k, src, dst, dev):
            self.c[k] = send(src, dst, rs_send.at[self.s, k], rs_recv.at[self.s, k], dev)

        def w(self, *ks):
            for k in ks:
                self.c[k].wait_recv()

        def first(self):
            s = self.s
            pt = part.at[s]
            self.go(0, pt.at[qO, A1], rhla.at[s, 1], dev_r)
            self.go(1, pt.at[qO, A2], rhra.at[s, 1], dev_l)
            self.go(2, pt.at[qO, B], rz.at[s, 2], dev_z)
            self.go(3, pt.at[pO, A1], rhla.at[s, 0], dev_r)
            self.go(4, pt.at[pO, A2], rhra.at[s, 0], dev_l)
            self.go(5, pt.at[qR, B], rz.at[s, 1], dev_z)
            self.go(6, pt.at[qL, B], rz.at[s, 3], dev_z)

        def mid_q(self):
            s = self.s
            pt = part.at[s]
            self.w(0)
            add_units(HA, lambda i: pt.at[qR, NB + i], lambda i: rhla.at[s, 1, i])
            self.go(8, pt.at[qR, A], rfla.at[s, 1], dev_r)
            self.w(1)
            add_units(NA - HA, lambda i: pt.at[qL, NB + HA + i], lambda i: rhra.at[s, 1, i])
            self.go(9, pt.at[qL, A], rfra.at[s, 1], dev_l)

        def opp_b(self):
            s = self.s
            pt = part.at[s]
            self.w(2)
            add_units(NB, lambda i: pt.at[pO, i], lambda i: rz.at[s, 2, i])
            self.go(10, pt.at[pO, B1], rhlb.at[s], dev_r)
            self.go(11, pt.at[pO, B2], rhrb.at[s], dev_l)

        def mid_p(self):
            s = self.s
            pt = part.at[s]
            self.w(3)
            add_units(HA, lambda i: pt.at[pR, NB + i], lambda i: rhla.at[s, 0, i])
            self.go(12, pt.at[pR, A], rfla.at[s, 0], dev_r)
            self.w(4)
            add_units(NA - HA, lambda i: pt.at[pL, NB + HA + i], lambda i: rhra.at[s, 0, i])
            self.go(13, pt.at[pL, A], rfra.at[s, 0], dev_l)

        def to_partner(self):
            s = self.s
            pt = part.at[s]
            self.w(8, 9)
            add_units(NA, lambda i: pt.at[qS, NB + i], lambda i: rfla.at[s, 1, i], lambda i: rfra.at[s, 1, i])
            self.go(16, pt.at[qS, A], rza.at[s], dev_z)
            self.go(7, pt.at[qS, B], rz.at[s, 0], dev_z)

        def mid_b(self):
            s = self.s
            pt = part.at[s]
            self.w(5, 10)
            add_units(HB, lambda i: pt.at[pR, i], lambda i: rz.at[s, 1, i], lambda i: rhlb.at[s, i])
            add_units(NB - HB, lambda i: pt.at[pR, HB + i], lambda i: rz.at[s, 1, HB + i])
            self.go(14, pt.at[pR, B], rflb.at[s], dev_r)
            self.w(6, 11)
            add_units(HB, lambda i: pt.at[pL, i], lambda i: rz.at[s, 3, i])
            add_units(NB - HB, lambda i: pt.at[pL, HB + i], lambda i: rz.at[s, 3, HB + i], lambda i: rhrb.at[s, i])
            self.go(15, pt.at[pL, B], rfrb.at[s], dev_l)

        def back(self, lo, hi):
            s = self.s

            def one(u, carry):
                gp, dev = peer(u, 1)
                pltpu.make_async_remote_copy(
                    part.at[s, pS, u], recv_out.at[s, g], g_send.at[s], g_recv.at[s],
                    device_id=dev, device_id_type=MESH).start()
                return carry

            lax.fori_loop(lo, hi, one, 0)

        def finish_a(self):
            s = self.s
            pt = part.at[s]
            self.w(12, 13, 16)
            add_units(NA, lambda i: pt.at[pS, NB + i], lambda i: rfla.at[s, 0, i], lambda i: rfra.at[s, 0, i], lambda i: rza.at[s, i])
            self.back(NB, G)

        def finish_b(self):
            s = self.s
            pt = part.at[s]
            self.w(7, 14, 15)
            add_units(NB, lambda i: pt.at[pS, i], lambda i: rz.at[s, 0, i], lambda i: rflb.at[s, i], lambda i: rfrb.at[s, i])
            self.back(1, NB)
            pltpu.make_async_copy(part.at[s, pS, 0], recv_out.at[s, g], own_sem.at[s]).start()

        def done(self):
            s = self.s
            bytes_of(G - 1, g_recv.at[s]).wait()
            pltpu.make_async_copy(part.at[s, pS, 0], recv_out.at[s, g], own_sem.at[s]).wait()

    def shard_of(p, h):
        return ((p // NX + h) % 2) * NX + p % NX

    def weight(s, p, h, m):
        return wfull[s, p, pl.ds(h * half, half), m].reshape(hrows, width)

    def forward(s, p, start=False):
        def one(j, carry):
            m, h = j // 2, j % 2
            got = lax.dot_general(weight(s, p, h, m), xg[m // 2, shard_of(p, h)], NT, preferred_element_type=F32)
            if start:
                acc[m, h] = got
            else:
                acc[m, h] += got
            return carry

        lax.fori_loop(0, 6, one, 0)

    def gates(s):
        lane = lax.broadcasted_iota(jnp.int32, (1, block), 1)
        live = lane < 0
        for b in range(batches):
            live = live | ((lane >= b * batch_rows) & (lane < b * batch_rows + counts_ref[s * batches + b]))
        tall = 32

        def one(j, carry):
            h = j // (hrows // tall)
            at = pl.ds(pl.multiple_of((j % (hrows // tall)) * tall, tall), tall)
            pre = acc[0, h, at, :]
            upv = acc[1, h, at, :]
            hg = jnp.where(live, acc[2, h, at, :], 0.0)
            sig = jax.nn.sigmoid(pre)
            act = pre * sig
            t3[0, h, at, :] = (hg * upv * sig * (1.0 + pre * (1.0 - sig))).astype(BF16)
            t3[1, h, at, :] = (hg * act).astype(BF16)
            t3[2, h, at, :] = jnp.where(live, act * upv, 0.0).astype(BF16)
            return carry

        lax.fori_loop(0, 2 * (hrows // tall), one, 0)

    scale = 1.0 / block

    def parts(s, p):
        def one(j, carry):
            m, h = j // 2, j % 2
            got = lax.dot_general(t3[m, h], xg[m // 2, shard_of(p, h)], NN, preferred_element_type=F32) * scale
            part[s, p, pl.ds(h * half, half), m] = got.astype(BF16).reshape(half, rows, width)
            return carry

        lax.fori_loop(0, 6, one, 0)

    def turn():
        def one(j, carry):
            gn[j // 2, j % 2] = t3[j // 2, j % 2].T
            return carry

        lax.fori_loop(0, 4, one, 0)

    def tg_copy(s, d):
        cols = pl.ds(pl.multiple_of(d * width, width), width)
        return pltpu.make_async_copy(tg.at[d], tg_out.at[pl.ds(s * block, block), cols], tg_sem.at[d])

    def token_grads(s, lo, hi):
        def one(d, carry):
            total = None
            for m in (0, 1):
                for h in (0, 1):
                    got = jnp.dot(gn[m, h], weight(s, shard_of(d, h), h, m), preferred_element_type=F32)
                    total = got if total is None else total + got
            tg[d] = total.astype(BF16)
            tg_copy(s, d).start()
            return carry

        lax.fori_loop(lo, hi, one, 0)

    def tg_wait(s):
        def one(d, carry):
            tg_copy(s, d).wait()
            return carry

        lax.fori_loop(0, 2 * NX, one, 0)

    g0, g1 = Gather(0), Gather(1)
    r0, r1 = Reduce(0), Reduce(1)

    spread(0)
    pick(1)
    g0.first()
    spread(1)
    wait_xg(0)
    forward(0, pS, start=True)
    g0.relay_b()
    g0.partner_a()
    g0.relay_a()
    forward(0, pL)
    forward(0, pR)
    g0.w(5)
    forward(0, qS)
    g0.opp_b()
    g0.relay_pa()
    g1.first()
    g0.w(10)
    forward(0, qL)
    g0.w(11)
    forward(0, qR)
    g0.w(12, 13)
    forward(0, pO)
    g0.w(14, 15, 16, 17)
    forward(0, qO)
    gates(0)
    g1.relay_b()
    g1.partner_a()
    parts(0, qO)
    parts(0, pO)
    parts(0, qR)
    parts(0, qL)
    g1.relay_a()
    parts(0, qS)
    parts(0, pR)
    parts(0, pL)
    parts(0, pS)
    load_xg(1)
    g1.opp_b()
    turn()
    token_grads(0, 0, 4)
    g1.relay_pa()
    r0.first()
    token_grads(0, 4, 8)
    wait_xg(1)
    forward(1, pS, start=True)
    forward(1, pL)
    forward(1, pR)
    g1.w(5)
    forward(1, qS)
    g1.w(10)
    forward(1, qL)
    g1.w(11)
    forward(1, qR)
    g1.w(12, 13)
    forward(1, pO)
    g1.w(14, 15, 16, 17)
    forward(1, qO)
    gates(1)
    r0.mid_q()
    r0.opp_b()
    r0.mid_p()
    parts(1, qO)
    parts(1, pO)
    r0.to_partner()
    parts(1, qR)
    parts(1, qL)
    r0.mid_b()
    r1.first()
    parts(1, qS)
    parts(1, pR)
    parts(1, pL)
    parts(1, pS)
    r0.finish_a()
    r0.finish_b()
    r1.mid_q()
    r1.opp_b()
    r1.mid_p()
    tg_wait(0)
    turn()
    r1.to_partner()
    token_grads(1, 0, 8)
    r1.mid_b()
    r1.finish_a()
    r1.finish_b()
    tg_wait(1)
    for copy in pending:
        copy.wait_send()
    for s in range(steps):
        bytes_of(G - 1, w_send.at[s]).wait()
        bytes_of(G - 1, g_send.at[s]).wait()
    r0.done()
    r1.done()


def home_kernel(assign_ref, recv_ref, tg_in, gate_ref, up_ref, down_ref, tg_out,
                recv, sums, tg, recv_sem, sum_sem, in_sem, out_sem):
    steps, count = recv.shape[:2]
    chunks = tg.shape[0]
    outs = (gate_ref, up_ref, down_ref)
    fetch = pltpu.make_async_copy(recv_ref, recv, recv_sem)
    fetch.start()
    tall = tg.shape[1]
    into = [pltpu.make_async_copy(tg_in.at[pl.ds(i * tall, tall)], tg.at[i], in_sem.at[i]) for i in range(chunks)]
    away = [pltpu.make_async_copy(tg.at[i], tg_out.at[pl.ds(i * tall, tall)], out_sem.at[i]) for i in range(chunks)]
    for copy in into:
        copy.start()
    sums[...] = jnp.zeros_like(sums)
    fetch.wait()
    share = chunks // len(outs)
    home = []
    for m, ref in enumerate(outs):
        for i in range(m * share, (m + 1) * share):
            into[i].wait()
            away[i].start()

        def one(i, carry):
            s, k = i // count, i % count
            sums[m, assign_ref[s, k]] += recv[s, k, m].astype(F32)
            return carry

        lax.fori_loop(0, steps * count, one, 0)
        home.append(pltpu.make_async_copy(sums.at[m], ref, sum_sem.at[m]))
        home[-1].start()
    for copy in home + away:
        copy.wait()


def local(tokens, upstream, counts, assign, gate_weight, up_weight, down_weight):
    steps, G = assign.shape
    batch_count = counts.shape[0] // steps
    block = tokens.shape[0] // steps
    experts, rows, width = gate_weight.shape
    dp_count = tokens.shape[1] // width
    NX = dp_count // 2
    NA = G - NB
    unit = (3, rows, width)

    def vm(*shape, dtype=BF16):
        return pltpu.VMEM(shape, dtype)

    dma = pltpu.SemaphoreType.DMA
    half = G // 2
    hrows = half * rows
    scratch = [
        vm(steps, G, *unit),
        vm(steps, dp_count, G, *unit),
        vm(steps, dp_count, G, *unit),
        vm(steps, 4, NB, *unit),
        vm(steps, 2, HA, *unit),
        vm(steps, HB, *unit),
        vm(steps, 2, NA - HA, *unit),
        vm(steps, NB - HB, *unit),
        vm(steps, 2, NA, *unit),
        vm(steps, NB, *unit),
        vm(steps, 2, NA, *unit),
        vm(steps, NB, *unit),
        vm(steps, NA, *unit),
        vm(2, dp_count, block, width),
        vm(3, 2, hrows, block, dtype=F32),
        vm(3, 2, hrows, block),
        vm(2, 2, block, hrows),
        vm(dp_count, block, width),
        dma((steps,)), dma((steps,)), dma((steps,)), dma((steps,)), dma((steps,)),
        dma((steps, 18)), dma((steps, 18)), dma((steps, 17)), dma((steps, 17)),
        dma((steps,)), dma((dp_count,)), dma((steps,)),
    ]
    vmem = pl.BlockSpec(memory_space=pltpu.VMEM)
    smem = pl.BlockSpec(memory_space=pltpu.SMEM)
    anyw = pl.BlockSpec(memory_space=pl.ANY)
    cfg = (G, NX, steps, block, rows, width, batch_count)
    flops = 2 * steps * 8 * block * (G * rows) * tokens.shape[1]
    token_grad, received = pl.pallas_call(
        functools.partial(fused_kernel, cfg),
        out_shape=(
            jax.ShapeDtypeStruct(tokens.shape, BF16),
            jax.ShapeDtypeStruct((steps, G, *unit), BF16),
        ),
        in_specs=[smem, smem, anyw, anyw, vmem, vmem, vmem],
        out_specs=(anyw, anyw),
        scratch_shapes=scratch,
        compiler_params=pltpu.CompilerParams(
            collective_id=0, has_side_effects=True, vmem_limit_bytes=VMEM_BYTES
        ),
        cost_estimate=pl.CostEstimate(flops=flops, bytes_accessed=6 * tokens.size, transcendentals=0),
        name="expert_step",
    )(assign, counts, tokens, upstream, gate_weight, up_weight, down_weight)

    grad = jax.ShapeDtypeStruct(gate_weight.shape, F32)
    chunks = 12
    return_grads = pl.pallas_call(
        home_kernel,
        out_shape=(grad, grad, grad, jax.ShapeDtypeStruct(tokens.shape, BF16)),
        in_specs=[smem, anyw, anyw],
        out_specs=(anyw, anyw, anyw, anyw),
        scratch_shapes=[
            vm(steps, G, *unit),
            vm(3, *gate_weight.shape, dtype=F32),
            vm(chunks, tokens.shape[0] // chunks, tokens.shape[1]),
            dma, dma((3,)), dma((chunks,)), dma((chunks,)),
        ],
        name="to_experts",
    )(assign, received, token_grad)
    return (return_grads[3], *return_grads[:3])


def solution(mesh):
    placed = (
        P(("dp", "expert"), None),
        P(("dp", "expert"), None),
        P(("dp", "expert")),
        P(),
        P(None, "expert", "dp"),
        P(None, "expert", "dp"),
        P(None, "expert", "dp"),
    )
    return jax.shard_map(
        local,
        mesh=mesh,
        in_specs=placed,
        out_specs=(
            P(("dp", "expert"), None),
            P(None, "expert", "dp"),
            P(None, "expert", "dp"),
            P(None, "expert", "dp"),
        ),
        check_vma=False,
    )
```

```python
import functools

import jax
import jax.numpy as jnp
from jax import lax
from jax.experimental import pallas as pl
from jax.experimental.pallas import tpu as pltpu
from jax.sharding import PartitionSpec as P

MESH = pl.DeviceIdType.MESH
F32 = jnp.float32
BF16 = jnp.bfloat16
NT = (((1,), (1,)), ((), ()))
NN = (((1,), (0,)), ((), ()))

NB = 7
N0 = 2
HAS = (5, 4)
HBS = (3, 4)
VMEM_BYTES = 55 * 2**20


def fused_kernel(cfg, assign_ref, counts_ref, tok_ref, ups_ref, gate_ref, up_ref, down_ref,
                 tg, recv_out,
                 stage, wfull, part, rz, rhla, rhlb, rhra, rhrb, rfla, rflb, rfra, rfrb, rza,
                 xg, acc, t3, gn,
                 w_send, w_recv_c, w_recv_b, w_recv_a, g_send, g_recv, ag_send, ag_recv, rs_send, rs_recv,
                 xg_sem):
    G, NX, steps, block, rows, width, batches = cfg
    units = G
    batch_rows = block // batches
    NA = units - NB
    half = units // 2
    hrows = half * rows
    dp = lax.axis_index("dp")
    g = lax.axis_index("expert")
    x = dp % NX
    z = dp // NX
    zh = g // half
    right = (x + 1) % NX
    left = (x + NX - 1) % NX
    opp = (x + 2) % NX
    zz = 1 - z
    pS, pL, pR, pO = z * NX + x, z * NX + left, z * NX + right, z * NX + opp
    qS, qL, qR, qO = zz * NX + x, zz * NX + left, zz * NX + right, zz * NX + opp
    dev_r = {"dp": pR, "expert": g}
    dev_l = {"dp": pL, "expert": g}
    dev_z = {"dp": qS, "expert": g}

    B = pl.ds(0, NB)
    BO = pl.ds(0, N0)
    BN = pl.ds(N0, NB - N0)
    A = pl.ds(NB, NA)
    B1 = [pl.ds(0, h) for h in HBS]
    B2 = [pl.ds(h, NB - h) for h in HBS]
    A1 = [pl.ds(NB, h) for h in HAS]
    A2 = [pl.ds(NB + h, NA - h) for h in HAS]

    NY = half // 2
    y = (g // 2) % NY
    core = g % 2

    def peer(u, sign):
        k = (u % half) // 2
        dy = k + (k // 2) * (5 - 2 * k)
        far = u // half
        yp = (y + sign * dy + NY) % NY
        gp = ((zh + far) % 2) * half + yp * 2 + (core + u) % 2
        return gp, {"dp": ((z + far) % 2) * NX + x, "expert": gp}

    barrier = pltpu.get_barrier_semaphore()

    def greet(j, carry):
        pl.semaphore_signal(barrier, inc=1, device_id=peer(j, 1)[1], device_id_type=MESH)
        return carry

    lax.fori_loop(1, G, greet, 0)
    for dev in (dev_r, dev_l, dev_z):
        pl.semaphore_signal(barrier, inc=1, device_id=dev, device_id_type=MESH)

    def load_xg(s):
        def one(d, carry):
            cols = pl.ds(pl.multiple_of(d * width, width), width)
            for k, ref in enumerate((tok_ref, ups_ref)):
                pltpu.make_async_copy(ref.at[pl.ds(s * block, block), cols], xg.at[k, d], xg_sem.at[s]).start()
            return carry

        lax.fori_loop(0, 2 * NX, one, 0)

    def wait_xg(s):
        pltpu.make_async_copy(xg, xg, xg_sem.at[s]).wait()

    load_xg(0)

    def pick(s):
        def one(i, carry):
            c = assign_ref[s, i]
            stage[s, i, 0] = gate_ref[c]
            stage[s, i, 1] = up_ref[c]
            stage[s, i, 2] = down_ref[c]
            return carry

        lax.fori_loop(0, G, one, 0)
        wfull[s, pS, 0] = stage[s, g]

    pick(0)
    pl.semaphore_wait(barrier, G - 1 + 3)

    def spread(s):
        def one(u, carry, recv):
            gp, dev = peer(u, -1)
            pltpu.make_async_remote_copy(
                stage.at[s, gp], wfull.at[s, dev["dp"], u], w_send.at[s], recv.at[s],
                device_id=dev, device_id_type=MESH).start()
            return carry

        lax.fori_loop(1, N0, functools.partial(one, recv=w_recv_c), 0)
        lax.fori_loop(N0, NB, functools.partial(one, recv=w_recv_b), 0)
        lax.fori_loop(NB, G, functools.partial(one, recv=w_recv_a), 0)

    def bytes_of(count, sem):
        some = stage.at[0, pl.ds(0, count)]
        return pltpu.make_async_copy(some, some, sem)

    pending = []

    def send(src, dst, ssem, rsem, dev):
        copy = pltpu.make_async_remote_copy(src, dst, ssem, rsem, device_id=dev, device_id_type=MESH)
        copy.start()
        pending.append(copy)
        return copy

    class Gather:
        def __init__(self, s):
            self.s = s
            self.c = {}

        def go(self, k, p, piece, dev):
            ref = wfull.at[self.s, p, piece]
            self.c[k] = send(ref, ref, ag_send.at[self.s, k], ag_recv.at[self.s, k], dev)

        def first(self):
            bytes_of(N0 - 1, w_recv_c.at[self.s]).wait()
            self.go(0, pS, BO, dev_r)
            self.go(1, pS, BO, dev_l)
            self.go(5, pS, BO, dev_z)
            bytes_of(NB - N0, w_recv_b.at[self.s]).wait()
            self.go(18, pS, BN, dev_r)
            self.go(19, pS, BN, dev_l)
            self.go(20, pS, BN, dev_z)
            bytes_of(NA, w_recv_a.at[self.s]).wait()
            self.go(2, pS, A, dev_z)
            self.go(3, pS, A, dev_r)
            self.go(4, pS, A, dev_l)

        def w(self, *ks):
            for k in ks:
                self.c[k].wait_recv()

        def relay_b(self):
            self.w(0, 18)
            self.go(6, pL, B1[self.s], dev_r)
            self.go(10, pL, B, dev_z)
            self.w(1, 19)
            self.go(7, pR, B2[self.s], dev_l)
            self.go(11, pR, B, dev_z)

        def partner_a(self):
            self.w(2)
            self.go(8, qS, A, dev_r)
            self.go(9, qS, A, dev_l)

        def relay_a(self):
            self.w(3)
            self.go(12, pL, A1[self.s], dev_r)
            self.w(4)
            self.go(13, pR, A2[self.s], dev_l)

        def opp_b(self):
            self.w(6)
            self.go(16, pO, B1[self.s], dev_z)
            self.w(7)
            self.go(17, pO, B2[self.s], dev_z)

        def relay_pa(self):
            self.w(8)
            self.go(14, qL, A1[self.s], dev_r)
            self.w(9)
            self.go(15, qR, A2[self.s], dev_l)

    def add_into(dst, *others):
        total = dst[...].astype(F32)
        for o in others:
            total = total + o[...].astype(F32)
        dst[...] = total.astype(BF16)

    def add_units(n, dst, *others):
        def one(i, carry):
            add_into(dst(i), *[o(i) for o in others])
            return carry

        lax.fori_loop(0, n, one, 0)

    class Reduce:
        def __init__(self, s):
            self.s = s
            self.c = {}
            self.pt = part.at[s]
            self.ha, self.hb = HAS[s], HBS[s]
            self.rha = [(rhla.at[s, k, pl.ds(0, self.ha)], rhra.at[s, k, pl.ds(0, NA - self.ha)]) for k in (0, 1)]
            self.rhb = (rhlb.at[s, pl.ds(0, self.hb)], rhrb.at[s, pl.ds(0, NB - self.hb)])

        def go(self, k, src, dst, dev):
            self.c[k] = send(src, dst, rs_send.at[self.s, k], rs_recv.at[self.s, k], dev)

        def w(self, *ks):
            for k in ks:
                self.c[k].wait_recv()

        def first(self):
            s, pt = self.s, self.pt
            self.go(0, pt.at[qO, A1[s]], self.rha[1][0], dev_r)
            self.go(1, pt.at[qO, A2[s]], self.rha[1][1], dev_l)
            self.go(2, pt.at[qO, B], rz.at[s, 2], dev_z)
            self.go(3, pt.at[pO, A1[s]], self.rha[0][0], dev_r)
            self.go(4, pt.at[pO, A2[s]], self.rha[0][1], dev_l)
            self.go(5, pt.at[qR, B], rz.at[s, 1], dev_z)
            self.go(6, pt.at[qL, B], rz.at[s, 3], dev_z)

        def mid_a(self, k, near, far, row, kr, kl, into_r, into_l):
            s, pt = self.s, self.pt
            self.w(near)
            add_units(self.ha, lambda i: pt.at[into_r, NB + i], lambda i: rhla.at[s, k, i])
            self.go(kr, pt.at[into_r, A], rfla.at[s, k], dev_r)
            self.w(far)
            add_units(NA - self.ha, lambda i: pt.at[into_l, NB + self.ha + i], lambda i: rhra.at[s, k, i])
            self.go(kl, pt.at[into_l, A], rfra.at[s, k], dev_l)

        def mid_q(self):
            self.mid_a(1, 0, 1, None, 8, 9, qR, qL)

        def mid_p(self):
            self.mid_a(0, 3, 4, None, 12, 13, pR, pL)

        def opp_b(self):
            s, pt = self.s, self.pt
            self.w(2)
            add_units(NB, lambda i: pt.at[pO, i], lambda i: rz.at[s, 2, i])
            self.go(10, pt.at[pO, B1[s]], self.rhb[0], dev_r)
            self.go(11, pt.at[pO, B2[s]], self.rhb[1], dev_l)

        def to_partner(self):
            s, pt = self.s, self.pt
            self.w(8, 9)
            add_units(NA, lambda i: pt.at[qS, NB + i], lambda i: rfla.at[s, 1, i], lambda i: rfra.at[s, 1, i])
            self.go(16, pt.at[qS, A], rza.at[s], dev_z)
            self.go(7, pt.at[qS, BN], rz.at[s, 0, BN], dev_z)
            self.go(17, pt.at[qS, BO], rz.at[s, 0, BO], dev_z)

        def mid_b(self):
            s, pt, hb = self.s, self.pt, self.hb
            self.w(5, 10)
            add_units(hb, lambda i: pt.at[pR, i], lambda i: rz.at[s, 1, i], lambda i: rhlb.at[s, i])
            add_units(NB - hb, lambda i: pt.at[pR, hb + i], lambda i: rz.at[s, 1, hb + i])
            self.go(14, pt.at[pR, BN], rflb.at[s, BN], dev_r)
            self.w(6, 11)
            add_units(hb, lambda i: pt.at[pL, i], lambda i: rz.at[s, 3, i])
            add_units(NB - hb, lambda i: pt.at[pL, hb + i], lambda i: rz.at[s, 3, hb + i], lambda i: rhrb.at[s, i])
            self.go(15, pt.at[pL, BN], rfrb.at[s, BN], dev_l)
            self.go(18, pt.at[pR, BO], rflb.at[s, BO], dev_r)
            self.go(19, pt.at[pL, BO], rfrb.at[s, BO], dev_l)

        def back(self, lo, hi):
            s = self.s

            def one(u, carry):
                gp, dev = peer(u, 1)
                pltpu.make_async_remote_copy(
                    part.at[s, pS, u], recv_out.at[s, g], g_send.at[s], g_recv.at[s],
                    device_id=dev, device_id_type=MESH).start()
                return carry

            lax.fori_loop(lo, hi, one, 0)

        def finish_a(self):
            s, pt = self.s, self.pt
            self.w(12, 13, 16)
            add_units(NA, lambda i: pt.at[pS, NB + i], lambda i: rfla.at[s, 0, i], lambda i: rfra.at[s, 0, i], lambda i: rza.at[s, i])
            self.back(NB, G)

        def finish_b(self):
            s, pt = self.s, self.pt

            def total(lo, n):
                add_units(n, lambda i: pt.at[pS, lo + i], lambda i: rz.at[s, 0, lo + i], lambda i: rflb.at[s, lo + i], lambda i: rfrb.at[s, lo + i])

            self.w(7, 14, 15)
            total(N0, NB - N0)
            self.back(N0, NB)
            self.w(17, 18, 19)
            total(0, N0)
            self.back(1, N0)
            recv_out[s, g] = part[s, pS, 0]

        def done(self):
            bytes_of(G - 1, g_recv.at[self.s]).wait()

    def shard_of(p, h):
        return ((p // NX + h) % 2) * NX + p % NX

    def weight(s, p, h, m):
        return wfull[s, p, pl.ds(h * half, half), m].reshape(hrows, width)

    def forward(s, p, start=False):
        def one(j, carry):
            m, h = j // 2, j % 2
            got = lax.dot_general(weight(s, p, h, m), xg[m // 2, shard_of(p, h)], NT, preferred_element_type=F32)
            if start:
                acc[m, h] = got
            else:
                acc[m, h] += got
            return carry

        lax.fori_loop(0, 6, one, 0)

    def gates(s):
        lane = lax.broadcasted_iota(jnp.int32, (1, block), 1)
        live = lane < 0
        for b in range(batches):
            live = live | ((lane >= b * batch_rows) & (lane < b * batch_rows + counts_ref[s * batches + b]))
        tall = 32

        def one(j, carry):
            h = j // (hrows // tall)
            at = pl.ds(pl.multiple_of((j % (hrows // tall)) * tall, tall), tall)
            pre = acc[0, h, at, :]
            upv = acc[1, h, at, :]
            hg = jnp.where(live, acc[2, h, at, :], 0.0)
            sig = jax.nn.sigmoid(pre)
            act = pre * sig
            t3[0, h, at, :] = (hg * upv * sig * (1.0 + pre * (1.0 - sig))).astype(BF16)
            t3[1, h, at, :] = (hg * act).astype(BF16)
            t3[2, h, at, :] = jnp.where(live, act * upv, 0.0).astype(BF16)
            return carry

        lax.fori_loop(0, 2 * (hrows // tall), one, 0)

    scale = 1.0 / block

    def parts(s, p):
        def one(j, carry):
            m, h = j // 2, j % 2
            got = lax.dot_general(t3[m, h], xg[m // 2, shard_of(p, h)], NN, preferred_element_type=F32) * scale
            part[s, p, pl.ds(h * half, half), m] = got.astype(BF16).reshape(half, rows, width)
            return carry

        lax.fori_loop(0, 6, one, 0)

    def turn():
        def one(j, carry):
            gn[j // 2, j % 2] = t3[j // 2, j % 2].T
            return carry

        lax.fori_loop(0, 4, one, 0)

    def token_grads(s, lo, hi):
        def one(d, carry):
            total = None
            for m in (0, 1):
                for h in (0, 1):
                    got = jnp.dot(gn[m, h], weight(s, shard_of(d, h), h, m), preferred_element_type=F32)
                    total = got if total is None else total + got
            tg[s, d] = total.astype(BF16)
            return carry

        lax.fori_loop(lo, hi, one, 0)

    g0, g1 = Gather(0), Gather(1)
    r0, r1 = Reduce(0), Reduce(1)

    spread(0)
    pick(1)
    g0.first()
    spread(1)
    wait_xg(0)
    forward(0, pS, start=True)
    g0.relay_b()
    g0.partner_a()
    g0.relay_a()
    forward(0, pL)
    forward(0, pR)
    g0.w(5, 20)
    forward(0, qS)
    g0.opp_b()
    g0.relay_pa()
    g1.first()
    g0.w(10)
    forward(0, qL)
    g0.w(11)
    forward(0, qR)
    g0.w(12, 13)
    forward(0, pO)
    g0.w(14, 15, 16, 17)
    forward(0, qO)
    gates(0)
    g1.relay_b()
    g1.partner_a()
    parts(0, qO)
    parts(0, pO)
    parts(0, qR)
    parts(0, qL)
    g1.relay_a()
    parts(0, qS)
    parts(0, pR)
    parts(0, pL)
    parts(0, pS)
    load_xg(1)
    g1.opp_b()
    turn()
    token_grads(0, 0, 4)
    g1.relay_pa()
    r0.first()
    token_grads(0, 4, 8)
    wait_xg(1)
    forward(1, pS, start=True)
    forward(1, pL)
    forward(1, pR)
    g1.w(5, 20)
    forward(1, qS)
    g1.w(10)
    forward(1, qL)
    g1.w(11)
    forward(1, qR)
    g1.w(12, 13)
    forward(1, pO)
    g1.w(14, 15, 16, 17)
    forward(1, qO)
    gates(1)
    r0.mid_q()
    r0.opp_b()
    r0.mid_p()
    parts(1, qO)
    parts(1, pO)
    r0.to_partner()
    parts(1, qR)
    parts(1, qL)
    r0.mid_b()
    r1.first()
    parts(1, qS)
    parts(1, pR)
    parts(1, pL)
    parts(1, pS)
    r0.finish_a()
    r0.finish_b()
    r1.mid_q()
    r1.opp_b()
    r1.mid_p()
    turn()
    r1.to_partner()
    token_grads(1, 0, 8)
    r1.mid_b()
    r1.finish_a()
    r1.finish_b()
    for copy in pending:
        copy.wait_send()
    for s in range(steps):
        bytes_of(G - 1, w_send.at[s]).wait()
        bytes_of(G - 1, g_send.at[s]).wait()
    r0.done()
    r1.done()


def home_kernel(assign_ref, recv, tg, gate_ref, up_ref, down_ref, tg_out, sums, sum_sem, out_sem):
    steps, count = recv.shape[:2]
    pieces, block, width = tg.shape[1:]
    outs = (gate_ref, up_ref, down_ref)
    away = []
    for i in range(steps * pieces):
        s, d = i // pieces, i % pieces
        to = tg_out.at[pl.ds(s * block, block), pl.ds(d * width, width)]
        away.append(pltpu.make_async_copy(tg.at[s, d], to, out_sem.at[i]))
        away[-1].start()
    sums[...] = jnp.zeros_like(sums)
    for m, ref in enumerate(outs):
        def one(i, carry):
            s, k = i // count, i % count
            sums[m, assign_ref[s, k]] += recv[s, k, m].astype(F32)
            return carry

        lax.fori_loop(0, steps * count, one, 0)
        away.append(pltpu.make_async_copy(sums.at[m], ref, sum_sem.at[m]))
        away[-1].start()
    for copy in away:
        copy.wait()


def local(tokens, upstream, counts, assign, gate_weight, up_weight, down_weight):
    steps, G = assign.shape
    batch_count = counts.shape[0] // steps
    block = tokens.shape[0] // steps
    experts, rows, width = gate_weight.shape
    dp_count = tokens.shape[1] // width
    NX = dp_count // 2
    NA = G - NB
    unit = (3, rows, width)

    def vm(*shape, dtype=BF16):
        return pltpu.VMEM(shape, dtype)

    dma = pltpu.SemaphoreType.DMA
    half = G // 2
    hrows = half * rows
    scratch = [
        vm(steps, G, *unit),
        vm(steps, dp_count, G, *unit),
        vm(steps, dp_count, G, *unit),
        vm(steps, 4, NB, *unit),
        vm(steps, 2, max(HAS), *unit),
        vm(steps, max(HBS), *unit),
        vm(steps, 2, NA - min(HAS), *unit),
        vm(steps, NB - min(HBS), *unit),
        vm(steps, 2, NA, *unit),
        vm(steps, NB, *unit),
        vm(steps, 2, NA, *unit),
        vm(steps, NB, *unit),
        vm(steps, NA, *unit),
        vm(2, dp_count, block, width),
        vm(3, 2, hrows, block, dtype=F32),
        vm(3, 2, hrows, block),
        vm(2, 2, block, hrows),
        dma((steps,)), dma((steps,)), dma((steps,)), dma((steps,)), dma((steps,)), dma((steps,)),
        dma((steps, 21)), dma((steps, 21)), dma((steps, 20)), dma((steps, 20)),
        dma((steps,)),
    ]
    vmem = pl.BlockSpec(memory_space=pltpu.VMEM)
    smem = pl.BlockSpec(memory_space=pltpu.SMEM)
    anyw = pl.BlockSpec(memory_space=pl.ANY)
    cfg = (G, NX, steps, block, rows, width, batch_count)
    flops = 2 * steps * 8 * block * (G * rows) * tokens.shape[1]
    token_grad, received = pl.pallas_call(
        functools.partial(fused_kernel, cfg),
        out_shape=(
            pltpu.VMEM((steps, dp_count, block, width), BF16),
            pltpu.VMEM((steps, G, *unit), BF16),
        ),
        in_specs=[smem, smem, anyw, anyw, vmem, vmem, vmem],
        out_specs=(vmem, vmem),
        scratch_shapes=scratch,
        compiler_params=pltpu.CompilerParams(
            collective_id=0, has_side_effects=True, vmem_limit_bytes=VMEM_BYTES
        ),
        cost_estimate=pl.CostEstimate(flops=flops, bytes_accessed=6 * tokens.size, transcendentals=0),
        name="expert_step",
    )(assign, counts, tokens, upstream, gate_weight, up_weight, down_weight)

    grad = jax.ShapeDtypeStruct(gate_weight.shape, F32)
    in_vmem = functools.partial(pltpu.with_memory_space_constraint, memory_space=pltpu.VMEM)
    return_grads = pl.pallas_call(
        home_kernel,
        out_shape=(grad, grad, grad, jax.ShapeDtypeStruct(tokens.shape, BF16)),
        in_specs=[smem, vmem, vmem],
        out_specs=(anyw, anyw, anyw, anyw),
        scratch_shapes=[
            vm(3, *gate_weight.shape, dtype=F32),
            dma((3,)), dma((steps * dp_count,)),
        ],
        compiler_params=pltpu.CompilerParams(vmem_limit_bytes=16 * 2**20),
        name="to_experts",
    )(assign, in_vmem(received), in_vmem(token_grad))
    return (return_grads[3], *return_grads[:3])


def solution(mesh):
    placed = (
        P(("dp", "expert"), None),
        P(("dp", "expert"), None),
        P(("dp", "expert")),
        P(),
        P(None, "expert", "dp"),
        P(None, "expert", "dp"),
        P(None, "expert", "dp"),
    )
    return jax.shard_map(
        local,
        mesh=mesh,
        in_specs=placed,
        out_specs=(
            P(("dp", "expert"), None),
            P(None, "expert", "dp"),
            P(None, "expert", "dp"),
            P(None, "expert", "dp"),
        ),
        check_vma=False,
    )
```

```python
import functools

import jax
import jax.numpy as jnp
from jax import lax
from jax.experimental import pallas as pl
from jax.experimental.pallas import tpu as pltpu
from jax.sharding import PartitionSpec as P

MESH = pl.DeviceIdType.MESH
F32 = jnp.float32
BF16 = jnp.bfloat16
NT = (((1,), (1,)), ((), ()))
NN = (((1,), (0,)), ((), ()))

NB = 7
N0 = 2
BGROUPS = (((0, 2), (2, 6), (6, 7)), ((0, 7),))
AGROUPS = (((7, 10), (10, 16)), ((7, 16),))
HAS = (5, 4)
HBS = (3, 4)
VMEM_BYTES = 55 * 2**20


def fused_kernel(cfg, assign_ref, counts_ref, tok_ref, ups_ref, gate_ref, up_ref, down_ref,
                 tg, recv_out,
                 stage, wfull, part, rz, rhla, rhlb, rhra, rhrb, rfla, rflb, rfra, rfrb, rza,
                 xg, acc, t3, gn,
                 w_send, w_recv, g_send, g_recv, ag_send, ag_recv, rs_send, rs_recv,
                 xg_sem, own, own_sem):
    G, NX, steps, block, rows, width, batches = cfg
    units = G
    batch_rows = block // batches
    NA = units - NB
    half = units // 2
    hrows = half * rows
    dp = lax.axis_index("dp")
    g = lax.axis_index("expert")
    x = dp % NX
    z = dp // NX
    zh = g // half
    right = (x + 1) % NX
    left = (x + NX - 1) % NX
    opp = (x + 2) % NX
    zz = 1 - z
    pS, pL, pR, pO = z * NX + x, z * NX + left, z * NX + right, z * NX + opp
    qS, qL, qR, qO = zz * NX + x, zz * NX + left, zz * NX + right, zz * NX + opp
    dev_r = {"dp": pR, "expert": g}
    dev_l = {"dp": pL, "expert": g}
    dev_z = {"dp": qS, "expert": g}

    B = pl.ds(0, NB)
    BO = pl.ds(0, N0)
    BN = pl.ds(N0, NB - N0)
    A = pl.ds(NB, NA)
    B1 = [pl.ds(0, h) for h in HBS]
    B2 = [pl.ds(h, NB - h) for h in HBS]
    A1 = [pl.ds(NB, h) for h in HAS]
    A2 = [pl.ds(NB + h, NA - h) for h in HAS]

    NY = half // 2
    y = (g // 2) % NY
    core = g % 2

    def peer(u, sign):
        k = (u % half) // 2
        dy = k + (k // 2) * (5 - 2 * k)
        far = u // half
        yp = (y + sign * dy + NY) % NY
        gp = ((zh + far) % 2) * half + yp * 2 + (core + u) % 2
        return gp, {"dp": ((z + far) % 2) * NX + x, "expert": gp}

    barrier = pltpu.get_barrier_semaphore()
    shards = [pltpu.make_async_copy(ref, own.at[m], own_sem.at[m]) for m, ref in enumerate((gate_ref, up_ref, down_ref))]
    for copy in shards:
        copy.start()

    def greet(j, carry):
        pl.semaphore_signal(barrier, inc=1, device_id=peer(j, 1)[1], device_id_type=MESH)
        return carry

    lax.fori_loop(1, G, greet, 0)
    for dev in (dev_r, dev_l, dev_z):
        pl.semaphore_signal(barrier, inc=1, device_id=dev, device_id_type=MESH)

    def load_xg(s):
        def one(d, carry):
            cols = pl.ds(pl.multiple_of(d * width, width), width)
            for k, ref in enumerate((tok_ref, ups_ref)):
                pltpu.make_async_copy(ref.at[pl.ds(s * block, block), cols], xg.at[k, d], xg_sem.at[s]).start()
            return carry

        lax.fori_loop(0, 2 * NX, one, 0)

    def wait_xg(s):
        pltpu.make_async_copy(xg, xg, xg_sem.at[s]).wait()

    def pick(s):
        def one(i, carry):
            c = assign_ref[s, i]
            for m in range(3):
                stage[s, i, m] = own[m, c]
            return carry

        lax.fori_loop(0, G, one, 0)
        wfull[s, pS, 0] = stage[s, g]

    for copy in shards:
        copy.wait()
    pick(0)
    load_xg(0)
    pl.semaphore_wait(barrier, G - 1 + 3)

    def spread(s):
        def one(u, carry, recv):
            gp, dev = peer(u, -1)
            pltpu.make_async_remote_copy(
                stage.at[s, gp], wfull.at[s, dev["dp"], u], w_send.at[s], recv.at[s],
                device_id=dev, device_id_type=MESH).start()
            return carry

        for i, (lo, hi) in enumerate(BGROUPS[s] + AGROUPS[s]):
            lax.fori_loop(max(lo, 1), hi, functools.partial(one, recv=w_recv.at[i]), 0)

    def arrived(s, i):
        lo, hi = (BGROUPS[s] + AGROUPS[s])[i]
        bytes_of(hi - max(lo, 1), w_recv.at[i, s]).wait()

    def bytes_of(count, sem):
        some = stage.at[0, pl.ds(0, count)]
        return pltpu.make_async_copy(some, some, sem)

    pending = []

    def send(src, dst, ssem, rsem, dev):
        copy = pltpu.make_async_remote_copy(src, dst, ssem, rsem, device_id=dev, device_id_type=MESH)
        copy.start()
        pending.append(copy)
        return copy

    class Gather:
        def __init__(self, s):
            self.s = s
            self.c = {}

        def go(self, k, p, piece, dev):
            n = len(self.c)
            ref = wfull.at[self.s, p, piece]
            self.c[k] = send(ref, ref, ag_send.at[self.s, n], ag_recv.at[self.s, n], dev)

        def first(self):
            s = self.s
            count = len(BGROUPS[s])
            for i, (lo, hi) in enumerate(BGROUPS[s]):
                arrived(s, i)
                for k, dev in (("br", dev_r), ("bl", dev_l), ("bz", dev_z)):
                    self.go((k, i), pS, pl.ds(lo, hi - lo), dev)
            for i, (lo, hi) in enumerate(AGROUPS[s]):
                arrived(s, count + i)
                for k, dev in (("az", dev_z), ("ar", dev_r), ("al", dev_l)):
                    self.go((k, i), pS, pl.ds(lo, hi - lo), dev)

        def first_ready(self):
            s = self.s
            for i in range(len(BGROUPS[s]) + len(AGROUPS[s])):
                arrived(s, i)
            self.go(("az", 0), pS, A, dev_z)
            self.go(("br", 0), pS, B, dev_r)
            self.go(("bl", 0), pS, B, dev_l)
            self.go(("ar", 0), pS, A, dev_r)
            self.go(("al", 0), pS, A, dev_l)
            self.go(("bz", 0), pS, B, dev_z)

        def all_of(self, kind):
            self.w(*[k for k in self.c if isinstance(k, tuple) and k[0] == kind])

        def w(self, *ks):
            for k in ks:
                self.c[k].wait_recv()

        def relay_b(self):
            self.all_of("br")
            self.go(6, pL, B1[self.s], dev_r)
            self.go(10, pL, B, dev_z)
            self.all_of("bl")
            self.go(7, pR, B2[self.s], dev_l)
            self.go(11, pR, B, dev_z)

        def partner_a(self):
            self.all_of("az")
            self.go(8, qS, A, dev_r)
            self.go(9, qS, A, dev_l)

        def relay_a(self):
            self.all_of("ar")
            self.go(12, pL, A1[self.s], dev_r)
            self.all_of("al")
            self.go(13, pR, A2[self.s], dev_l)

        def opp_b(self):
            self.w(6)
            self.go(16, pO, B1[self.s], dev_z)
            self.w(7)
            self.go(17, pO, B2[self.s], dev_z)

        def relay_pa(self):
            self.w(8)
            self.go(14, qL, A1[self.s], dev_r)
            self.w(9)
            self.go(15, qR, A2[self.s], dev_l)

    def add_into(dst, *others):
        total = dst[...].astype(F32)
        for o in others:
            total = total + o[...].astype(F32)
        dst[...] = total.astype(BF16)

    def add_units(n, dst, *others):
        def one(i, carry):
            add_into(dst(i), *[o(i) for o in others])
            return carry

        lax.fori_loop(0, n, one, 0)

    class Reduce:
        def __init__(self, s):
            self.s = s
            self.c = {}
            self.pt = part.at[s]
            self.ha, self.hb = HAS[s], HBS[s]
            self.rha = [(rhla.at[s, k, pl.ds(0, self.ha)], rhra.at[s, k, pl.ds(0, NA - self.ha)]) for k in (0, 1)]
            self.rhb = (rhlb.at[s, pl.ds(0, self.hb)], rhrb.at[s, pl.ds(0, NB - self.hb)])

        def go(self, k, src, dst, dev):
            self.c[k] = send(src, dst, rs_send.at[self.s, k], rs_recv.at[self.s, k], dev)

        def w(self, *ks):
            for k in ks:
                self.c[k].wait_recv()

        def first(self):
            s, pt = self.s, self.pt
            self.go(0, pt.at[qO, A1[s]], self.rha[1][0], dev_r)
            self.go(1, pt.at[qO, A2[s]], self.rha[1][1], dev_l)
            self.go(2, pt.at[qO, B], rz.at[s, 2], dev_z)
            self.go(3, pt.at[pO, A1[s]], self.rha[0][0], dev_r)
            self.go(4, pt.at[pO, A2[s]], self.rha[0][1], dev_l)
            self.go(5, pt.at[qR, B], rz.at[s, 1], dev_z)
            self.go(6, pt.at[qL, B], rz.at[s, 3], dev_z)

        def mid_a(self, k, near, far, row, kr, kl, into_r, into_l):
            s, pt = self.s, self.pt
            self.w(near)
            add_units(self.ha, lambda i: pt.at[into_r, NB + i], lambda i: rhla.at[s, k, i])
            self.go(kr, pt.at[into_r, A], rfla.at[s, k], dev_r)
            self.w(far)
            add_units(NA - self.ha, lambda i: pt.at[into_l, NB + self.ha + i], lambda i: rhra.at[s, k, i])
            self.go(kl, pt.at[into_l, A], rfra.at[s, k], dev_l)

        def mid_q(self):
            self.mid_a(1, 0, 1, None, 8, 9, qR, qL)

        def mid_p(self):
            self.mid_a(0, 3, 4, None, 12, 13, pR, pL)

        def opp_b(self):
            s, pt = self.s, self.pt
            self.w(2)
            add_units(NB, lambda i: pt.at[pO, i], lambda i: rz.at[s, 2, i])
            self.go(10, pt.at[pO, B1[s]], self.rhb[0], dev_r)
            self.go(11, pt.at[pO, B2[s]], self.rhb[1], dev_l)

        def to_partner(self):
            s, pt = self.s, self.pt
            self.w(8, 9)
            add_units(NA, lambda i: pt.at[qS, NB + i], lambda i: rfla.at[s, 1, i], lambda i: rfra.at[s, 1, i])
            self.go(16, pt.at[qS, A], rza.at[s], dev_z)
            self.go(7, pt.at[qS, BN], rz.at[s, 0, BN], dev_z)
            self.go(17, pt.at[qS, BO], rz.at[s, 0, BO], dev_z)

        def mid_b(self):
            s, pt, hb = self.s, self.pt, self.hb
            self.w(5, 10)
            add_units(hb, lambda i: pt.at[pR, i], lambda i: rz.at[s, 1, i], lambda i: rhlb.at[s, i])
            add_units(NB - hb, lambda i: pt.at[pR, hb + i], lambda i: rz.at[s, 1, hb + i])
            self.go(14, pt.at[pR, BN], rflb.at[s, BN], dev_r)
            self.w(6, 11)
            add_units(hb, lambda i: pt.at[pL, i], lambda i: rz.at[s, 3, i])
            add_units(NB - hb, lambda i: pt.at[pL, hb + i], lambda i: rz.at[s, 3, hb + i], lambda i: rhrb.at[s, i])
            self.go(15, pt.at[pL, BN], rfrb.at[s, BN], dev_l)
            self.go(18, pt.at[pR, BO], rflb.at[s, BO], dev_r)
            self.go(19, pt.at[pL, BO], rfrb.at[s, BO], dev_l)

        def back(self, lo, hi):
            s = self.s

            def one(u, carry):
                gp, dev = peer(u, 1)
                pltpu.make_async_remote_copy(
                    part.at[s, pS, u], recv_out.at[s, g], g_send.at[s], g_recv.at[s],
                    device_id=dev, device_id_type=MESH).start()
                return carry

            lax.fori_loop(lo, hi, one, 0)

        def finish_a(self):
            s, pt = self.s, self.pt
            self.w(12, 13, 16)
            add_units(NA, lambda i: pt.at[pS, NB + i], lambda i: rfla.at[s, 0, i], lambda i: rfra.at[s, 0, i], lambda i: rza.at[s, i])
            self.back(NB, G)

        def finish_b(self):
            s, pt = self.s, self.pt

            def total(lo, n):
                add_units(n, lambda i: pt.at[pS, lo + i], lambda i: rz.at[s, 0, lo + i], lambda i: rflb.at[s, lo + i], lambda i: rfrb.at[s, lo + i])

            self.w(7, 14, 15)
            total(N0, NB - N0)
            self.back(N0, NB)
            self.w(17, 18, 19)
            total(0, N0)
            self.back(1, N0)
            recv_out[s, g] = part[s, pS, 0]

        def done(self):
            bytes_of(G - 1, g_recv.at[self.s]).wait()

    def shard_of(p, h):
        return ((p // NX + h) % 2) * NX + p % NX

    def weight(s, p, h, m):
        return wfull[s, p, pl.ds(h * half, half), m].reshape(hrows, width)

    def forward(s, p, start=False):
        def one(j, carry):
            m, h = j // 2, j % 2
            got = lax.dot_general(weight(s, p, h, m), xg[m // 2, shard_of(p, h)], NT, preferred_element_type=F32)
            if start:
                acc[m, h] = got
            else:
                acc[m, h] += got
            return carry

        lax.fori_loop(0, 6, one, 0)

    def gates(s):
        lane = lax.broadcasted_iota(jnp.int32, (1, block), 1)
        live = lane < 0
        for b in range(batches):
            live = live | ((lane >= b * batch_rows) & (lane < b * batch_rows + counts_ref[s * batches + b]))
        tall = 32

        def one(j, carry):
            h = j // (hrows // tall)
            at = pl.ds(pl.multiple_of((j % (hrows // tall)) * tall, tall), tall)
            pre = acc[0, h, at, :]
            upv = acc[1, h, at, :]
            hg = jnp.where(live, acc[2, h, at, :], 0.0)
            sig = jax.nn.sigmoid(pre)
            act = pre * sig
            t3[0, h, at, :] = (hg * upv * sig * (1.0 + pre * (1.0 - sig))).astype(BF16)
            t3[1, h, at, :] = (hg * act).astype(BF16)
            t3[2, h, at, :] = jnp.where(live, act * upv, 0.0).astype(BF16)
            return carry

        lax.fori_loop(0, 2 * (hrows // tall), one, 0)

    scale = 1.0 / block

    def parts(s, p):
        def one(j, carry):
            m, h = j // 2, j % 2
            got = lax.dot_general(t3[m, h], xg[m // 2, shard_of(p, h)], NN, preferred_element_type=F32) * scale
            part[s, p, pl.ds(h * half, half), m] = got.astype(BF16).reshape(half, rows, width)
            return carry

        lax.fori_loop(0, 6, one, 0)

    def turn():
        def one(j, carry):
            gn[j // 2, j % 2] = t3[j // 2, j % 2].T
            return carry

        lax.fori_loop(0, 4, one, 0)

    def token_grads(s, lo, hi):
        def one(d, carry):
            total = None
            for m in (0, 1):
                for h in (0, 1):
                    got = jnp.dot(gn[m, h], weight(s, shard_of(d, h), h, m), preferred_element_type=F32)
                    total = got if total is None else total + got
            tg[s, d] = total.astype(BF16)
            return carry

        lax.fori_loop(lo, hi, one, 0)

    g0, g1 = Gather(0), Gather(1)
    r0, r1 = Reduce(0), Reduce(1)

    spread(0)
    pick(1)
    g0.first()
    spread(1)
    wait_xg(0)
    forward(0, pS, start=True)
    g0.relay_b()
    g0.partner_a()
    g0.relay_a()
    forward(0, pL)
    forward(0, pR)
    g0.all_of("bz")
    forward(0, qS)
    g0.opp_b()
    g0.relay_pa()
    g1.first_ready()
    g0.w(10)
    forward(0, qL)
    g0.w(11)
    forward(0, qR)
    g0.w(12, 13)
    forward(0, pO)
    g0.w(14, 15, 16, 17)
    forward(0, qO)
    gates(0)
    g1.relay_b()
    g1.partner_a()
    parts(0, qO)
    parts(0, pO)
    parts(0, qR)
    parts(0, qL)
    g1.relay_a()
    parts(0, qS)
    parts(0, pR)
    parts(0, pL)
    parts(0, pS)
    load_xg(1)
    g1.opp_b()
    turn()
    token_grads(0, 0, 4)
    g1.relay_pa()
    r0.first()
    token_grads(0, 4, 8)
    wait_xg(1)
    forward(1, pS, start=True)
    forward(1, pL)
    forward(1, pR)
    g1.all_of("bz")
    forward(1, qS)
    g1.w(10)
    forward(1, qL)
    g1.w(11)
    forward(1, qR)
    g1.w(12, 13)
    forward(1, pO)
    g1.w(14, 15, 16, 17)
    forward(1, qO)
    gates(1)
    r0.mid_q()
    r0.opp_b()
    r0.mid_p()
    parts(1, qO)
    parts(1, pO)
    r0.to_partner()
    parts(1, qR)
    parts(1, qL)
    r0.mid_b()
    r1.first()
    parts(1, qS)
    parts(1, pR)
    parts(1, pL)
    parts(1, pS)
    r0.finish_a()
    r0.finish_b()
    r1.mid_q()
    r1.opp_b()
    r1.mid_p()
    turn()
    r1.to_partner()
    token_grads(1, 0, 8)
    r1.mid_b()
    r1.finish_a()
    r1.finish_b()
    for copy in pending:
        copy.wait_send()
    for s in range(steps):
        bytes_of(G - 1, w_send.at[s]).wait()
        bytes_of(G - 1, g_send.at[s]).wait()
    r0.done()
    r1.done()


def home_kernel(assign_ref, recv, tg, gate_ref, up_ref, down_ref, tg_out, sums, sum_sem, out_sem):
    steps, count = recv.shape[:2]
    pieces, block, width = tg.shape[1:]
    outs = (gate_ref, up_ref, down_ref)
    away = []
    for i in range(steps * pieces):
        s, d = i // pieces, i % pieces
        to = tg_out.at[pl.ds(s * block, block), pl.ds(d * width, width)]
        away.append(pltpu.make_async_copy(tg.at[s, d], to, out_sem.at[i]))
        away[-1].start()
    sums[...] = jnp.zeros_like(sums)
    for m, ref in enumerate(outs):
        def one(i, carry):
            s, k = i // count, i % count
            sums[m, assign_ref[s, k]] += recv[s, k, m].astype(F32)
            return carry

        lax.fori_loop(0, steps * count, one, 0, unroll=4)
        away.append(pltpu.make_async_copy(sums.at[m], ref, sum_sem.at[m]))
        away[-1].start()
    for copy in away:
        copy.wait()


def local(tokens, upstream, counts, assign, gate_weight, up_weight, down_weight):
    steps, G = assign.shape
    batch_count = counts.shape[0] // steps
    block = tokens.shape[0] // steps
    experts, rows, width = gate_weight.shape
    dp_count = tokens.shape[1] // width
    NX = dp_count // 2
    NA = G - NB
    unit = (3, rows, width)

    def vm(*shape, dtype=BF16):
        return pltpu.VMEM(shape, dtype)

    dma = pltpu.SemaphoreType.DMA
    half = G // 2
    hrows = half * rows
    scratch = [
        vm(steps, G, *unit),
        vm(steps, dp_count, G, *unit),
        vm(steps, dp_count, G, *unit),
        vm(steps, 4, NB, *unit),
        vm(steps, 2, max(HAS), *unit),
        vm(steps, max(HBS), *unit),
        vm(steps, 2, NA - min(HAS), *unit),
        vm(steps, NB - min(HBS), *unit),
        vm(steps, 2, NA, *unit),
        vm(steps, NB, *unit),
        vm(steps, 2, NA, *unit),
        vm(steps, NB, *unit),
        vm(steps, NA, *unit),
        vm(2, dp_count, block, width),
        vm(3, 2, hrows, block, dtype=F32),
        vm(3, 2, hrows, block),
        vm(2, 2, block, hrows),
        dma((steps,)), dma((5, steps)), dma((steps,)), dma((steps,)),
        dma((steps, 27)), dma((steps, 27)), dma((steps, 20)), dma((steps, 20)),
        dma((steps,)),
        vm(3, *gate_weight.shape), dma((3,)),
    ]
    vmem = pl.BlockSpec(memory_space=pltpu.VMEM)
    smem = pl.BlockSpec(memory_space=pltpu.SMEM)
    anyw = pl.BlockSpec(memory_space=pl.ANY)
    cfg = (G, NX, steps, block, rows, width, batch_count)
    flops = 2 * steps * 8 * block * (G * rows) * tokens.shape[1]
    token_grad, received = pl.pallas_call(
        functools.partial(fused_kernel, cfg),
        out_shape=(
            pltpu.VMEM((steps, dp_count, block, width), BF16),
            pltpu.VMEM((steps, G, *unit), BF16),
        ),
        in_specs=[smem, smem, anyw, anyw, anyw, anyw, anyw],
        out_specs=(vmem, vmem),
        scratch_shapes=scratch,
        compiler_params=pltpu.CompilerParams(
            collective_id=0, has_side_effects=True, vmem_limit_bytes=VMEM_BYTES
        ),
        cost_estimate=pl.CostEstimate(flops=flops, bytes_accessed=6 * tokens.size, transcendentals=0),
        name="expert_step",
    )(assign, counts, tokens, upstream, gate_weight, up_weight, down_weight)

    grad = jax.ShapeDtypeStruct(gate_weight.shape, F32)
    in_vmem = functools.partial(pltpu.with_memory_space_constraint, memory_space=pltpu.VMEM)
    return_grads = pl.pallas_call(
        home_kernel,
        out_shape=(grad, grad, grad, jax.ShapeDtypeStruct(tokens.shape, BF16)),
        in_specs=[smem, vmem, vmem],
        out_specs=(anyw, anyw, anyw, anyw),
        scratch_shapes=[
            vm(3, *gate_weight.shape, dtype=F32),
            dma((3,)), dma((steps * dp_count,)),
        ],
        compiler_params=pltpu.CompilerParams(vmem_limit_bytes=16 * 2**20),
        name="to_experts",
    )(assign, in_vmem(received), in_vmem(token_grad))
    return (return_grads[3], *return_grads[:3])


def solution(mesh):
    placed = (
        P(("dp", "expert"), None),
        P(("dp", "expert"), None),
        P(("dp", "expert")),
        P(),
        P(None, "expert", "dp"),
        P(None, "expert", "dp"),
        P(None, "expert", "dp"),
    )
    return jax.shard_map(
        local,
        mesh=mesh,
        in_specs=placed,
        out_specs=(
            P(("dp", "expert"), None),
            P(None, "expert", "dp"),
            P(None, "expert", "dp"),
            P(None, "expert", "dp"),
        ),
        check_vma=False,
    )
```

```python
import functools

import jax
import jax.numpy as jnp
from jax import lax
from jax.experimental import pallas as pl
from jax.experimental.pallas import tpu as pltpu
from jax.sharding import PartitionSpec as P

MESH = pl.DeviceIdType.MESH
F32 = jnp.float32
BF16 = jnp.bfloat16
NT = (((1,), (1,)), ((), ()))
NN = (((1,), (0,)), ((), ()))

NB = 7
N0 = 2
BGROUPS = (((0, 2), (2, 6), (6, 7)), ((0, 7),))
AGROUPS = (((7, 10), (10, 16)), ((7, 16),))
HAS = (5, 4)
HBS = (3, 4)
VMEM_BYTES = 55 * 2**20


def fused_kernel(cfg, assign_ref, counts_ref, tok_ref, ups_ref, gate_ref, up_ref, down_ref,
                 tg, recv_out,
                 stage, wfull, part, rz, rhla, rhlb, rhra, rhrb, rfla, rflb, rfra, rfrb, rza,
                 xg, acc, t3, gn,
                 w_send, w_recv, g_send, g_recv, ag_send, ag_recv, rs_send, rs_recv,
                 xg_sem, own, own_sem):
    G, NX, steps, block, rows, width, batches = cfg
    units = G
    batch_rows = block // batches
    NA = units - NB
    half = units // 2
    hrows = half * rows
    dp = lax.axis_index("dp")
    g = lax.axis_index("expert")
    x = dp % NX
    z = dp // NX
    zh = g // half
    right = (x + 1) % NX
    left = (x + NX - 1) % NX
    opp = (x + 2) % NX
    zz = 1 - z
    pS, pL, pR, pO = z * NX + x, z * NX + left, z * NX + right, z * NX + opp
    qS, qL, qR, qO = zz * NX + x, zz * NX + left, zz * NX + right, zz * NX + opp
    dev_r = {"dp": pR, "expert": g}
    dev_l = {"dp": pL, "expert": g}
    dev_z = {"dp": qS, "expert": g}

    B = pl.ds(0, NB)
    BO = pl.ds(0, N0)
    BN = pl.ds(N0, NB - N0)
    A = pl.ds(NB, NA)
    B1 = [pl.ds(0, h) for h in HBS]
    B2 = [pl.ds(h, NB - h) for h in HBS]
    A1 = [pl.ds(NB, h) for h in HAS]
    A2 = [pl.ds(NB + h, NA - h) for h in HAS]

    NY = half // 2
    y = (g // 2) % NY
    core = g % 2

    def peer(u, sign):
        k = (u % half) // 2
        dy = k + (k // 2) * (5 - 2 * k)
        far = u // half
        yp = (y + sign * dy + NY) % NY
        gp = ((zh + far) % 2) * half + yp * 2 + (core + u) % 2
        return gp, {"dp": ((z + far) % 2) * NX + x, "expert": gp}

    barrier = pltpu.get_barrier_semaphore()
    shards = [pltpu.make_async_copy(ref, own.at[m], own_sem.at[m]) for m, ref in enumerate((gate_ref, up_ref, down_ref))]
    for copy in shards:
        copy.start()

    def greet(j, carry):
        pl.semaphore_signal(barrier, inc=1, device_id=peer(j, 1)[1], device_id_type=MESH)
        return carry

    lax.fori_loop(1, G, greet, 0)
    for dev in (dev_r, dev_l, dev_z):
        pl.semaphore_signal(barrier, inc=1, device_id=dev, device_id_type=MESH)

    def load_xg(s):
        def one(d, carry):
            cols = pl.ds(pl.multiple_of(d * width, width), width)
            for k, ref in enumerate((tok_ref, ups_ref)):
                pltpu.make_async_copy(ref.at[pl.ds(s * block, block), cols], xg.at[k, d], xg_sem.at[s]).start()
            return carry

        lax.fori_loop(0, 2 * NX, one, 0)

    def wait_xg(s):
        pltpu.make_async_copy(xg, xg, xg_sem.at[s]).wait()

    def pick(s):
        def one(i, carry):
            c = assign_ref[s, i]
            for m in range(3):
                stage[s, i, m] = own[m, c]
            return carry

        lax.fori_loop(0, G, one, 0)
        wfull[s, pS, 0] = stage[s, g]

    for copy in shards:
        copy.wait()
    pick(0)
    load_xg(0)
    pl.semaphore_wait(barrier, G - 1 + 3)

    def spread(s):
        def one(u, carry, recv):
            gp, dev = peer(u, -1)
            pltpu.make_async_remote_copy(
                stage.at[s, gp], wfull.at[s, dev["dp"], u], w_send.at[s], recv.at[s],
                device_id=dev, device_id_type=MESH).start()
            return carry

        for i, (lo, hi) in enumerate(BGROUPS[s] + AGROUPS[s]):
            lax.fori_loop(max(lo, 1), hi, functools.partial(one, recv=w_recv.at[i]), 0)

    def arrived(s, i):
        lo, hi = (BGROUPS[s] + AGROUPS[s])[i]
        bytes_of(hi - max(lo, 1), w_recv.at[i, s]).wait()

    def bytes_of(count, sem):
        some = stage.at[0, pl.ds(0, count)]
        return pltpu.make_async_copy(some, some, sem)

    pending = []

    def send(src, dst, ssem, rsem, dev):
        copy = pltpu.make_async_remote_copy(src, dst, ssem, rsem, device_id=dev, device_id_type=MESH)
        copy.start()
        pending.append(copy)
        return copy

    class Gather:
        def __init__(self, s):
            self.s = s
            self.c = {}

        def go(self, k, p, piece, dev):
            n = len(self.c)
            ref = wfull.at[self.s, p, piece]
            self.c[k] = send(ref, ref, ag_send.at[self.s, n], ag_recv.at[self.s, n], dev)

        def first(self):
            s = self.s
            count = len(BGROUPS[s])
            for i, (lo, hi) in enumerate(BGROUPS[s]):
                arrived(s, i)
                for k, dev in (("br", dev_r), ("bl", dev_l), ("bz", dev_z)):
                    self.go((k, i), pS, pl.ds(lo, hi - lo), dev)
            for i, (lo, hi) in enumerate(AGROUPS[s]):
                arrived(s, count + i)
                for k, dev in (("az", dev_z), ("ar", dev_r), ("al", dev_l)):
                    self.go((k, i), pS, pl.ds(lo, hi - lo), dev)

        def first_ready(self):
            s = self.s
            for i in range(len(BGROUPS[s]) + len(AGROUPS[s])):
                arrived(s, i)
            self.go(("az", 0), pS, A, dev_z)
            self.go(("br", 0), pS, B, dev_r)
            self.go(("bl", 0), pS, B, dev_l)
            self.go(("ar", 0), pS, A, dev_r)
            self.go(("al", 0), pS, A, dev_l)
            self.go(("bz", 0), pS, B, dev_z)

        def all_of(self, kind):
            self.w(*[k for k in self.c if isinstance(k, tuple) and k[0] == kind])

        def w(self, *ks):
            for k in ks:
                self.c[k].wait_recv()

        def relay_b(self):
            self.all_of("br")
            self.go(6, pL, B1[self.s], dev_r)
            self.go(10, pL, B, dev_z)
            self.all_of("bl")
            self.go(7, pR, B2[self.s], dev_l)
            self.go(11, pR, B, dev_z)

        def partner_a(self):
            self.all_of("az")
            self.go(8, qS, A, dev_r)
            self.go(9, qS, A, dev_l)

        def relay_a(self):
            self.all_of("ar")
            self.go(12, pL, A1[self.s], dev_r)
            self.all_of("al")
            self.go(13, pR, A2[self.s], dev_l)

        def opp_b(self):
            self.w(6)
            self.go(16, pO, B1[self.s], dev_z)
            self.w(7)
            self.go(17, pO, B2[self.s], dev_z)

        def relay_pa(self):
            self.w(8)
            self.go(14, qL, A1[self.s], dev_r)
            self.w(9)
            self.go(15, qR, A2[self.s], dev_l)

    def add_into(dst, *others):
        total = dst[...].astype(F32)
        for o in others:
            total = total + o[...].astype(F32)
        dst[...] = total.astype(BF16)

    def add_units(n, dst, *others):
        def one(i, carry):
            add_into(dst(i), *[o(i) for o in others])
            return carry

        lax.fori_loop(0, n, one, 0)

    class Reduce:
        def __init__(self, s):
            self.s = s
            self.c = {}
            self.pt = part.at[s]
            self.ha, self.hb = HAS[s], HBS[s]
            self.rha = [(rhla.at[s, k, pl.ds(0, self.ha)], rhra.at[s, k, pl.ds(0, NA - self.ha)]) for k in (0, 1)]
            self.rhb = (rhlb.at[s, pl.ds(0, self.hb)], rhrb.at[s, pl.ds(0, NB - self.hb)])

        def go(self, k, src, dst, dev):
            self.c[k] = send(src, dst, rs_send.at[self.s, k], rs_recv.at[self.s, k], dev)

        def w(self, *ks):
            for k in ks:
                self.c[k].wait_recv()

        def first(self):
            s, pt = self.s, self.pt
            self.go(0, pt.at[qO, A1[s]], self.rha[1][0], dev_r)
            self.go(1, pt.at[qO, A2[s]], self.rha[1][1], dev_l)
            self.go(2, pt.at[qO, B], rz.at[s, 2], dev_z)
            self.go(3, pt.at[pO, A1[s]], self.rha[0][0], dev_r)
            self.go(4, pt.at[pO, A2[s]], self.rha[0][1], dev_l)
            self.go(5, pt.at[qR, B], rz.at[s, 1], dev_z)
            self.go(6, pt.at[qL, B], rz.at[s, 3], dev_z)

        def mid_a(self, k, near, far, row, kr, kl, into_r, into_l):
            s, pt = self.s, self.pt
            self.w(near)
            add_units(self.ha, lambda i: pt.at[into_r, NB + i], lambda i: rhla.at[s, k, i])
            self.go(kr, pt.at[into_r, A], rfla.at[s, k], dev_r)
            self.w(far)
            add_units(NA - self.ha, lambda i: pt.at[into_l, NB + self.ha + i], lambda i: rhra.at[s, k, i])
            self.go(kl, pt.at[into_l, A], rfra.at[s, k], dev_l)

        def mid_q(self):
            self.mid_a(1, 0, 1, None, 8, 9, qR, qL)

        def mid_p(self):
            self.mid_a(0, 3, 4, None, 12, 13, pR, pL)

        def opp_b(self):
            s, pt = self.s, self.pt
            self.w(2)
            add_units(NB, lambda i: pt.at[pO, i], lambda i: rz.at[s, 2, i])
            self.go(10, pt.at[pO, B1[s]], self.rhb[0], dev_r)
            self.go(11, pt.at[pO, B2[s]], self.rhb[1], dev_l)

        def to_partner(self):
            s, pt = self.s, self.pt
            self.w(8, 9)
            add_units(NA, lambda i: pt.at[qS, NB + i], lambda i: rfla.at[s, 1, i], lambda i: rfra.at[s, 1, i])
            self.go(16, pt.at[qS, A], rza.at[s], dev_z)
            self.go(7, pt.at[qS, BN], rz.at[s, 0, BN], dev_z)
            self.go(17, pt.at[qS, BO], rz.at[s, 0, BO], dev_z)

        def mid_b(self):
            s, pt, hb = self.s, self.pt, self.hb
            self.w(5, 10)
            add_units(hb, lambda i: pt.at[pR, i], lambda i: rz.at[s, 1, i], lambda i: rhlb.at[s, i])
            add_units(NB - hb, lambda i: pt.at[pR, hb + i], lambda i: rz.at[s, 1, hb + i])
            self.go(14, pt.at[pR, BN], rflb.at[s, BN], dev_r)
            self.w(6, 11)
            add_units(hb, lambda i: pt.at[pL, i], lambda i: rz.at[s, 3, i])
            add_units(NB - hb, lambda i: pt.at[pL, hb + i], lambda i: rz.at[s, 3, hb + i], lambda i: rhrb.at[s, i])
            self.go(15, pt.at[pL, BN], rfrb.at[s, BN], dev_l)
            self.go(18, pt.at[pR, BO], rflb.at[s, BO], dev_r)
            self.go(19, pt.at[pL, BO], rfrb.at[s, BO], dev_l)

        def back(self, lo, hi):
            s = self.s

            def one(u, carry):
                gp, dev = peer(u, 1)
                pltpu.make_async_remote_copy(
                    part.at[s, pS, u], recv_out.at[s, g], g_send.at[s], g_recv.at[s],
                    device_id=dev, device_id_type=MESH).start()
                return carry

            lax.fori_loop(lo, hi, one, 0)

        def finish_a(self):
            s, pt = self.s, self.pt
            self.w(12, 13, 16)
            add_units(NA, lambda i: pt.at[pS, NB + i], lambda i: rfla.at[s, 0, i], lambda i: rfra.at[s, 0, i], lambda i: rza.at[s, i])
            self.back(NB, G)

        def finish_b(self):
            s, pt = self.s, self.pt

            def total(lo, n):
                add_units(n, lambda i: pt.at[pS, lo + i], lambda i: rz.at[s, 0, lo + i], lambda i: rflb.at[s, lo + i], lambda i: rfrb.at[s, lo + i])

            self.w(7, 14, 15)
            total(N0, NB - N0)
            self.back(N0, NB)
            self.w(17, 18, 19)
            total(0, N0)
            self.back(1, N0)
            recv_out[s, g] = part[s, pS, 0]

        def done(self):
            bytes_of(G - 1, g_recv.at[self.s]).wait()

    def shard_of(p, h):
        return ((p // NX + h) % 2) * NX + p % NX

    def weight(s, p, h, m):
        return wfull[s, p, pl.ds(h * half, half), m].reshape(hrows, width)

    def forward(s, p, start=False):
        def one(j, carry):
            m, h = j // 2, j % 2
            got = lax.dot_general(weight(s, p, h, m), xg[m // 2, shard_of(p, h)], NT, preferred_element_type=F32)
            if start:
                acc[m, h] = got
            else:
                acc[m, h] += got
            return carry

        lax.fori_loop(0, 6, one, 0)

    def gates(s):
        lane = lax.broadcasted_iota(jnp.int32, (1, block), 1)
        live = lane < 0
        for b in range(batches):
            live = live | ((lane >= b * batch_rows) & (lane < b * batch_rows + counts_ref[s * batches + b]))
        tall = 32

        def one(j, carry):
            h = j // (hrows // tall)
            at = pl.ds(pl.multiple_of((j % (hrows // tall)) * tall, tall), tall)
            pre = acc[0, h, at, :]
            upv = acc[1, h, at, :]
            hg = jnp.where(live, acc[2, h, at, :], 0.0)
            sig = jax.nn.sigmoid(pre)
            act = pre * sig
            t3[0, h, at, :] = (hg * upv * sig * (1.0 + pre * (1.0 - sig))).astype(BF16)
            t3[1, h, at, :] = (hg * act).astype(BF16)
            t3[2, h, at, :] = jnp.where(live, act * upv, 0.0).astype(BF16)
            return carry

        lax.fori_loop(0, 2 * (hrows // tall), one, 0)

    scale = 1.0 / block

    def parts(s, p):
        def one(j, carry):
            m, h = j // 2, j % 2
            got = lax.dot_general(t3[m, h], xg[m // 2, shard_of(p, h)], NN, preferred_element_type=F32) * scale
            part[s, p, pl.ds(h * half, half), m] = got.astype(BF16).reshape(half, rows, width)
            return carry

        lax.fori_loop(0, 6, one, 0)

    def turn():
        def one(j, carry):
            gn[j // 2, j % 2] = t3[j // 2, j % 2].T
            return carry

        lax.fori_loop(0, 4, one, 0)

    def token_grads(s, lo, hi):
        def one(d, carry):
            total = None
            for m in (0, 1):
                for h in (0, 1):
                    got = jnp.dot(gn[m, h], weight(s, shard_of(d, h), h, m), preferred_element_type=F32)
                    total = got if total is None else total + got
            tg[s, d] = total.astype(BF16)
            return carry

        lax.fori_loop(lo, hi, one, 0)

    g0, g1 = Gather(0), Gather(1)
    r0, r1 = Reduce(0), Reduce(1)

    spread(0)
    g0.first()
    pick(1)
    spread(1)
    wait_xg(0)
    forward(0, pS, start=True)
    g0.relay_b()
    g0.partner_a()
    g0.relay_a()
    forward(0, pL)
    forward(0, pR)
    g0.all_of("bz")
    forward(0, qS)
    g0.opp_b()
    g0.relay_pa()
    g1.first_ready()
    g0.w(10)
    forward(0, qL)
    g0.w(11)
    forward(0, qR)
    g0.w(12, 13)
    forward(0, pO)
    g0.w(14, 15, 16, 17)
    forward(0, qO)
    gates(0)
    g1.relay_b()
    g1.partner_a()
    parts(0, qO)
    parts(0, pO)
    parts(0, qR)
    parts(0, qL)
    g1.relay_a()
    parts(0, qS)
    parts(0, pR)
    parts(0, pL)
    parts(0, pS)
    load_xg(1)
    g1.opp_b()
    turn()
    wait_xg(1)
    forward(1, pS, start=True)
    forward(1, pL)
    forward(1, pR)
    g1.all_of("bz")
    forward(1, qS)
    g1.relay_pa()
    r0.first()
    g1.w(10)
    forward(1, qL)
    g1.w(11)
    forward(1, qR)
    g1.w(12, 13)
    forward(1, pO)
    g1.w(14, 15, 16, 17)
    forward(1, qO)
    gates(1)
    r0.mid_q()
    r0.opp_b()
    r0.mid_p()
    parts(1, qO)
    parts(1, pO)
    token_grads(0, 0, 4)
    r0.to_partner()
    parts(1, qR)
    parts(1, qL)
    r0.mid_b()
    r1.first()
    parts(1, qS)
    parts(1, pR)
    parts(1, pL)
    parts(1, pS)
    token_grads(0, 4, 8)
    r0.finish_a()
    r0.finish_b()
    r1.mid_q()
    r1.opp_b()
    r1.mid_p()
    turn()
    r1.to_partner()
    token_grads(1, 0, 8)
    r1.mid_b()
    r1.finish_a()
    r1.finish_b()
    for copy in pending:
        copy.wait_send()
    for s in range(steps):
        bytes_of(G - 1, w_send.at[s]).wait()
        bytes_of(G - 1, g_send.at[s]).wait()
    r0.done()
    r1.done()


def home_kernel(assign_ref, recv, tg, gate_ref, up_ref, down_ref, tg_out, sums, sum_sem, out_sem):
    steps, count = recv.shape[:2]
    pieces, block, width = tg.shape[1:]
    outs = (gate_ref, up_ref, down_ref)
    away = []
    for i in range(steps * pieces):
        s, d = i // pieces, i % pieces
        to = tg_out.at[pl.ds(s * block, block), pl.ds(d * width, width)]
        away.append(pltpu.make_async_copy(tg.at[s, d], to, out_sem.at[i]))
        away[-1].start()
    sums[...] = jnp.zeros_like(sums)
    for m, ref in enumerate(outs):
        def one(i, carry):
            s, k = i // count, i % count
            sums[m, assign_ref[s, k]] += recv[s, k, m].astype(F32)
            return carry

        lax.fori_loop(0, steps * count, one, 0, unroll=4)
        away.append(pltpu.make_async_copy(sums.at[m], ref, sum_sem.at[m]))
        away[-1].start()
    for copy in away:
        copy.wait()


def local(tokens, upstream, counts, assign, gate_weight, up_weight, down_weight):
    steps, G = assign.shape
    batch_count = counts.shape[0] // steps
    block = tokens.shape[0] // steps
    experts, rows, width = gate_weight.shape
    dp_count = tokens.shape[1] // width
    NX = dp_count // 2
    NA = G - NB
    unit = (3, rows, width)

    def vm(*shape, dtype=BF16):
        return pltpu.VMEM(shape, dtype)

    dma = pltpu.SemaphoreType.DMA
    half = G // 2
    hrows = half * rows
    scratch = [
        vm(steps, G, *unit),
        vm(steps, dp_count, G, *unit),
        vm(steps, dp_count, G, *unit),
        vm(steps, 4, NB, *unit),
        vm(steps, 2, max(HAS), *unit),
        vm(steps, max(HBS), *unit),
        vm(steps, 2, NA - min(HAS), *unit),
        vm(steps, NB - min(HBS), *unit),
        vm(steps, 2, NA, *unit),
        vm(steps, NB, *unit),
        vm(steps, 2, NA, *unit),
        vm(steps, NB, *unit),
        vm(steps, NA, *unit),
        vm(2, dp_count, block, width),
        vm(3, 2, hrows, block, dtype=F32),
        vm(3, 2, hrows, block),
        vm(2, 2, block, hrows),
        dma((steps,)), dma((5, steps)), dma((steps,)), dma((steps,)),
        dma((steps, 27)), dma((steps, 27)), dma((steps, 20)), dma((steps, 20)),
        dma((steps,)),
        vm(3, *gate_weight.shape), dma((3,)),
    ]
    vmem = pl.BlockSpec(memory_space=pltpu.VMEM)
    smem = pl.BlockSpec(memory_space=pltpu.SMEM)
    anyw = pl.BlockSpec(memory_space=pl.ANY)
    cfg = (G, NX, steps, block, rows, width, batch_count)
    flops = 2 * steps * 8 * block * (G * rows) * tokens.shape[1]
    token_grad, received = pl.pallas_call(
        functools.partial(fused_kernel, cfg),
        out_shape=(
            pltpu.VMEM((steps, dp_count, block, width), BF16),
            pltpu.VMEM((steps, G, *unit), BF16),
        ),
        in_specs=[smem, smem, anyw, anyw, anyw, anyw, anyw],
        out_specs=(vmem, vmem),
        scratch_shapes=scratch,
        compiler_params=pltpu.CompilerParams(
            collective_id=0, has_side_effects=True, vmem_limit_bytes=VMEM_BYTES
        ),
        cost_estimate=pl.CostEstimate(flops=flops, bytes_accessed=6 * tokens.size, transcendentals=0),
        name="expert_step",
    )(assign, counts, tokens, upstream, gate_weight, up_weight, down_weight)

    grad = jax.ShapeDtypeStruct(gate_weight.shape, F32)
    in_vmem = functools.partial(pltpu.with_memory_space_constraint, memory_space=pltpu.VMEM)
    return_grads = pl.pallas_call(
        home_kernel,
        out_shape=(grad, grad, grad, jax.ShapeDtypeStruct(tokens.shape, BF16)),
        in_specs=[smem, vmem, vmem],
        out_specs=(anyw, anyw, anyw, anyw),
        scratch_shapes=[
            vm(3, *gate_weight.shape, dtype=F32),
            dma((3,)), dma((steps * dp_count,)),
        ],
        compiler_params=pltpu.CompilerParams(vmem_limit_bytes=16 * 2**20),
        name="to_experts",
    )(assign, in_vmem(received), in_vmem(token_grad))
    return (return_grads[3], *return_grads[:3])


def solution(mesh):
    placed = (
        P(("dp", "expert"), None),
        P(("dp", "expert"), None),
        P(("dp", "expert")),
        P(),
        P(None, "expert", "dp"),
        P(None, "expert", "dp"),
        P(None, "expert", "dp"),
    )
    return jax.shard_map(
        local,
        mesh=mesh,
        in_specs=placed,
        out_specs=(
            P(("dp", "expert"), None),
            P(None, "expert", "dp"),
            P(None, "expert", "dp"),
            P(None, "expert", "dp"),
        ),
        check_vma=False,
    )
```
